32 devices in a mesh: dp: 2 (over core), mp: 16 (over z, y, x).
Axes of the slice: x: 2, y: 2, z: 4, core: 2. Of those that a mesh axis runs over, the one named last changes fastest.
Arguments:
- inputs: bfloat16 [512, 4096], P('dp'), may hold values from -6 to 6
- upstream: bfloat16 [512, 4096], P('dp'), may hold values from -6 to 6
- eig_tiles: bfloat16 [16, 8, 8, 128, 128], P('mp'), may hold values from -0.09375 to 0.09375
- eigvals: float32 [4096], replicated, may hold values from 0.25 to 4
Outputs:
- grad_t: bfloat16 [4096, 512], P('mp', 'dp')
The draws below stay inside these ranges and needn't reach their ends.
All inputs are finite; a program needn't handle non-finite values.
Results may differ from the reference program's by a relative error of at most 0.013.
Values may be sent and summed in bfloat16 or wider, within the bound.
A program may use at most 64 MiB of HBM per device.

```python
import math
import jax
import jax.numpy as jnp
from jax import lax

D = 4096
TILE = 128
PR = 4
PC = 4
RT = 8
CT = 8
TOKENS = 512
N_MP = 16


def block_levels(stream_key, extent, split, low, high):
    factor_of = 1.0
    for axis_at, shards_of in split:
        steps = jax.random.uniform(jax.random.fold_in(jax.random.fold_in(stream_key, 6), axis_at), (shards_of,), jnp.float32, low / len(split), high / len(split))
        factor_of = factor_of * jnp.repeat(jnp.exp(steps), extent[axis_at] // shards_of).reshape((-1,) + (1,) * (len(extent) - 1 - axis_at))
    return factor_of


def normal_values(rng, extent, deviation, reach, split=(), kind=jnp.bfloat16):
    result = jax.random.normal(rng, extent, jnp.float32) * deviation
    if len(split) > 0:
        result = block_levels(rng, extent, split, -0.22, 0.18) * result
    return jnp.clip(result, min=-reach, max=reach).astype(kind)


def setup_inputs(seed: int = 0) -> dict:
    streams_of = jax.random.split(jax.random.key(seed), 5)
    inputs = normal_values(streams_of[0], (TOKENS, D), 1.0, 6.0, ((0, 2),))
    upstream = normal_values(streams_of[1], (TOKENS, D), 1.0, 6.0, ((0, 2),))
    eig_tiles = normal_values(streams_of[2], (N_MP, RT, CT, TILE, TILE), D ** -0.5, 0.09375, ((0, 16),))
    eigvals = jnp.clip(jnp.exp(jax.random.uniform(streams_of[3], (D,), jnp.float32, math.log(0.25), math.log(4.0))), 0.25, 4.0)
    return dict(inputs=inputs, upstream=upstream, eig_tiles=eig_tiles, eigvals=eigvals)


def reference(inputs, upstream, eig_tiles, eigvals):
    layout = eig_tiles.reshape(PR, PC, RT, CT, TILE, TILE)
    basis = jnp.transpose(layout, (2, 0, 4, 3, 1, 5)).reshape(D, D)
    proj_in = jnp.dot(inputs, basis, preferred_element_type=jnp.float32).astype(jnp.bfloat16)
    proj_up = jnp.dot(upstream, basis, preferred_element_type=jnp.float32).astype(jnp.bfloat16)
    gram = jnp.dot(proj_in.T, proj_up, preferred_element_type=jnp.float32)
    sym = 0.5 * (gram + gram.T)
    root = jnp.sqrt(eigvals)
    kernel = -1.0 / (root[:, None] * root[None, :] * (root[:, None] + root[None, :]))
    weighted = (kernel * sym).astype(jnp.bfloat16)
    mixed = jnp.dot(proj_in, weighted, preferred_element_type=jnp.float32)
    update = (proj_up.astype(jnp.float32) / root[None, :] + 2.0 / TOKENS * mixed).astype(jnp.bfloat16)
    grad_t = lax.dot_general(basis, update, (((1,), (1,)), ((), ())), preferred_element_type=jnp.float32)
    return grad_t.astype(jnp.bfloat16)
```

```python
import functools

import jax
import jax.numpy as jnp
from jax import lax
from jax.experimental import pallas as pl
from jax.experimental.pallas import tpu as pltpu
from jax.sharding import PartitionSpec as P


def kernel_of(left, right):
    root_left = jnp.sqrt(left)[:, None]
    root_right = jnp.sqrt(right)[None, :]
    return -1.0 / (root_left * root_right * (root_left + root_right))


def on_device(inputs, upstream, eig_tiles, eigvals):
    groups = lax.axis_size("mp")
    member = lax.axis_index("mp")
    width = eigvals.shape[0]
    slab = width // groups
    tile_rows = eig_tiles.shape[1]
    tile_cols = eig_tiles.shape[2]
    tile = eig_tiles.shape[3]
    grid_rows = width // (tile_rows * tile)
    grid_cols = groups // grid_rows
    piece = tile_cols * tile // groups
    local = jnp.transpose(eig_tiles[0], (0, 2, 1, 3)).reshape(tile_rows * tile, groups, piece)
    moved = lax.all_to_all(local, "mp", split_axis=1, concat_axis=1, tiled=True)
    moved = moved.reshape(tile_rows, tile, grid_rows, grid_cols, piece)
    basis = jnp.transpose(moved, (0, 2, 1, 3, 4)).reshape(width, slab)
    ordered = jnp.transpose(eigvals.reshape(tile_cols, grid_cols, tile), (1, 0, 2)).reshape(
        grid_cols, groups, piece
    )
    ordered = jnp.transpose(ordered, (1, 0, 2)).reshape(width)
    own = lax.dynamic_slice_in_dim(ordered, member * slab, slab)
    proj_in = jnp.dot(inputs, basis, preferred_element_type=jnp.float32).astype(jnp.bfloat16)
    proj_up = jnp.dot(upstream, basis, preferred_element_type=jnp.float32).astype(jnp.bfloat16)
    stacked = jnp.stack([proj_in, proj_up], 0)
    over_tokens = (((0,), (0,)), ((), ()))
    pieces = lax.all_gather(stacked, "mp", axis=2, tiled=True)
    part_in = pieces[0]
    part_up = pieces[1]
    block = lax.dot_general(proj_in, part_up, over_tokens, preferred_element_type=jnp.float32)
    block = block + lax.dot_general(
        proj_up, part_in, over_tokens, preferred_element_type=jnp.float32
    )
    joined = jnp.concatenate([block, part_in.astype(jnp.float32)], 0)
    gram = joined[:slab]
    all_in = joined[slab:].astype(jnp.bfloat16)
    total = lax.psum(gram.astype(jnp.bfloat16), "dp").astype(jnp.float32)
    weighted = (kernel_of(own, ordered) * (0.5 * total)).astype(jnp.bfloat16)
    over_columns = (((1,), (1,)), ((), ()))
    mixed = lax.dot_general(all_in, weighted, over_columns, preferred_element_type=jnp.float32)
    factor = 2.0 / (lax.axis_size("dp") * inputs.shape[0])
    update = (proj_up.astype(jnp.float32) / jnp.sqrt(own)[None, :] + factor * mixed).astype(
        jnp.bfloat16
    )
    own_rows = lax.all_to_all(basis, "mp", split_axis=0, concat_axis=1, tiled=True)
    every_update = lax.all_gather(update, "mp", axis=1, tiled=True)
    result = lax.dot_general(
        own_rows, every_update, over_columns, preferred_element_type=jnp.float32
    )
    return result.astype(jnp.bfloat16)


def line_kernel(
    dims, ev, x_in, x_up, eig, out,
    ub, xb, pf, sup, sdn, rup, rdn, gz, gp, kb, so, ss, sr, mx, ms, mr, uz, ff, fs, fb,
    ld_u, ld_x, up_s, up_r, dn_s, dn_r, zu_s, zd_s, z_r, p_s, p_r, c_s, c_r,
    m_s, m_r, wu_s, wd_s, w_r, f_s, f_r,
):
    R, C, tr, tc, tile, slab, factor = dims
    q = slab // tile
    n = R * C
    rows = tr * tile
    d = lax.axis_index("dp")
    me = lax.axis_index("mp")
    r = me // C
    c = me % C
    partner = (1 - d, me)
    above = (d, (me + C) % n)
    below = (d, (me + n - C) % n)
    f32, bf16 = jnp.float32, jnp.bfloat16

    def remote(src, dst, s_sem, r_sem, dev):
        return pltpu.make_async_remote_copy(
            src_ref=src, dst_ref=dst, send_sem=s_sem, recv_sem=r_sem,
            device_id=dev, device_id_type=pl.DeviceIdType.MESH,
        )

    def arrived(dst, r_sem):
        remote(dst, dst, c_s.at[0, 0], r_sem, partner).wait_recv()

    def left(src, s_sem):
        remote(src, src, s_sem, c_r.at[0, 0], partner).wait_send()

    for h, x in enumerate((x_in, x_up)):
        for la in range(tr):
            col = pl.multiple_of((la * R + r) * tile, tile)
            pltpu.make_async_copy(
                x.at[:, pl.ds(col, tile)], xb.at[h, :, la * tile:(la + 1) * tile], ld_x.at[h]
            ).start()
        if h == 0:
            for t in [R - 1, 0] + list(range(R - 2, 0, -1)):
                for k in range(q):
                    for la in range(tr):
                        pltpu.make_async_copy(
                            eig.at[0, la, t * q + k],
                            ub.at[t, la * tile:(la + 1) * tile, k * tile:(k + 1) * tile],
                            ld_u.at[t],
                        ).start()
    barrier = pltpu.get_barrier_semaphore()
    for k in range(1, n):
        pl.semaphore_signal(
            barrier, inc=1, device_id=(d, (me + k) % n), device_id_type=pl.DeviceIdType.MESH
        )
    pl.semaphore_signal(
        barrier, inc=1, device_id=partner, device_id_type=pl.DeviceIdType.MESH
    )
    pl.semaphore_wait(barrier, n)

    for h in range(2):
        pltpu.make_async_copy(xb.at[h], xb.at[h], ld_x.at[h]).wait()
        for t in [R - 1, 0] + list(range(R - 2, 0, -1)):
            if h == 0:
                pltpu.make_async_copy(ub.at[t], ub.at[t], ld_u.at[t]).wait()
            pf[h, t] = jnp.dot(xb[h], ub[t], preferred_element_type=f32)
            if t > 0:
                @pl.when(r == 0)
                def _():
                    sup[h, t] = pf[h, t].astype(bf16)
                    remote(sup.at[h, t], rup.at[h, t], up_s.at[h, t], up_r.at[h, t], above).start()
            if t < R - 1:
                @pl.when(r == R - 1)
                def _():
                    sdn[h, t] = pf[h, t].astype(bf16)
                    remote(sdn.at[h, t], rdn.at[h, t], dn_s.at[h, t], dn_r.at[h, t], below).start()

    def kernel_rows(lb, carry):
        row = jnp.sqrt(ev[pl.ds(lb * C + c, 1), :])
        sj = jnp.broadcast_to(row, (tile, tile)).T
        t = lb // q
        at = pl.multiple_of((lb % q) * tile, tile)
        for cc in range(C):
            for k in range(q):
                si = jnp.sqrt(ev[pl.ds((r * q + k) * C + cc, 1), :])
                kb[t, cc, pl.ds(at, tile), k * tile:(k + 1) * tile] = -0.5 / (si * sj * (si + sj))
        return carry

    lax.fori_loop(0, tc, kernel_rows, 0)

    def relay_up(h):
        for t in range(R - 1, 0, -1):
            @pl.when((r > 0) & (r < t))
            def _():
                arrived(rup.at[h, t], up_r.at[h, t])
                sup[h, t] = (pf[h, t] + rup[h, t].astype(f32)).astype(bf16)
                remote(sup.at[h, t], rup.at[h, t], up_s.at[h, t], up_r.at[h, t], above).start()

    def relay_down(h):
        for t in range(R - 1):
            @pl.when((r < R - 1) & (r > t))
            def _():
                arrived(rdn.at[h, t], dn_r.at[h, t])
                sdn[h, t] = (pf[h, t] + rdn[h, t].astype(f32)).astype(bf16)
                remote(sdn.at[h, t], rdn.at[h, t], dn_s.at[h, t], dn_r.at[h, t], below).start()

    for h in range(2):
        @pl.when(r < R // 2)
        def _():
            relay_up(h)
            relay_down(h)

        @pl.when(r >= R // 2)
        def _():
            relay_down(h)
            relay_up(h)

        for t in range(R):
            @pl.when(r == t)
            def _():
                total = pf[h, t]
                if t > 0:
                    arrived(rup.at[h, t], up_r.at[h, t])
                    total = total + rup[h, t].astype(f32)
                if t < R - 1:
                    arrived(rdn.at[h, t], dn_r.at[h, t])
                    total = total + rdn[h, t].astype(f32)
                total = total.astype(bf16)
                gz[h, t] = total
                if t < R - 1:
                    remote(gz.at[h, t], gz.at[h, t], zu_s.at[h, t], z_r.at[h, t], above).start()
                if t > 0:
                    remote(gz.at[h, t], gz.at[h, t], zd_s.at[h, t], z_r.at[h, t], below).start()
                gp[h, c] = total
        for k in range(1, C):
            cc = (c + k) % C
            remote(
                gp.at[h, c], gp.at[h, c], p_s.at[h, k], p_r.at[h, c], (d, r * C + cc)
            ).start()

    def each_piece(body):
        body(r, None)
        for k in range(1, R):
            @pl.when(r >= k)
            def _():
                body(r - k, True)

            @pl.when(r + k < R)
            def _():
                body(r + k, False)

    def relay(buf, s, from_below, s_up, s_dn, r_sem):
        arrived(buf, r_sem)
        if from_below:
            @pl.when(r < R - 1)
            def _():
                remote(buf, buf, s_up, r_sem, above).start()
        else:
            @pl.when(r > 0)
            def _():
                remote(buf, buf, s_dn, r_sem, below).start()

    tokens_both = (((0,), (0,)), ((), ()))

    def gram_piece(s, from_below):
        if from_below is not None:
            for h in range(2):
                relay(
                    gz.at[h, s], s, from_below, zu_s.at[h, s], zd_s.at[h, s], z_r.at[h, s]
                )

        def one(cc, carry):
            block = lax.dot_general(gz[1, s], gp[0, cc], tokens_both, preferred_element_type=f32)
            block = block + lax.dot_general(
                gz[0, s], gp[1, cc], tokens_both, preferred_element_type=f32
            )
            so[s, cc] = block
            ss[s, cc] = block.astype(bf16)
            remote(ss.at[s, cc], sr.at[s, cc], c_s.at[s, cc], c_r.at[s, cc], partner).start()
            return carry

        lax.fori_loop(0, C, one, 0)

    for h in range(2):
        for k in range(1, C):
            cc = (c + k) % C
            arrived(gp.at[h, cc], p_r.at[h, cc])
    each_piece(gram_piece)

    mx[...] = jnp.zeros_like(mx)

    def mixed_piece(s, carry):
        def one(cc, carry):
            arrived(sr.at[s, cc], c_r.at[s, cc])
            weighted = (kb[s, cc] * (so[s, cc] + sr[s, cc].astype(f32))).astype(bf16)
            mx[cc] += jnp.dot(gz[0, s], weighted, preferred_element_type=f32)
            return carry

        return lax.fori_loop(0, C, one, carry)

    lax.fori_loop(0, R, lambda k, carry: mixed_piece((r + k) % R, carry), 0)

    for k in range(1, C):
        cc = (c + k) % C
        ms[cc] = mx[cc].astype(bf16)
        remote(ms.at[cc], mr.at[c], m_s.at[cc], m_r.at[c], (d, r * C + cc)).start()
    total = mx[c]
    for k in range(1, C):
        cc = (c + k) % C
        arrived(mr.at[cc], m_r.at[cc])
        total = total + mr[cc].astype(f32)
    roots = jnp.concatenate(
        [jnp.sqrt(ev[pl.ds((r * q + k) * C + c, 1), :]) for k in range(q)], axis=1
    )
    uz[r] = (gz[1, r].astype(f32) / roots + factor * total).astype(bf16)

    @pl.when(r < R - 1)
    def _():
        remote(uz.at[r], uz.at[r], wu_s.at[r], w_r.at[r], above).start()

    @pl.when(r > 0)
    def _():
        remote(uz.at[r], uz.at[r], wd_s.at[r], w_r.at[r], below).start()

    ff[...] = jnp.zeros_like(ff)
    chunks = rows // slab

    def grad_piece(s, from_below):
        if from_below is not None:
            relay(uz.at[s], s, from_below, wu_s.at[s], wd_s.at[s], w_r.at[s])

        def one(i, carry):
            at = pl.multiple_of(i * slab, slab)
            ff[i] += lax.dot_general(
                ub[s, pl.ds(at, slab), :], uz[s], (((1,), (1,)), ((), ())),
                preferred_element_type=f32,
            )
            return carry

        lax.fori_loop(0, chunks, one, 0)

    each_piece(grad_piece)

    for la in range(tr):
        g = la * R + r
        owner = g // q
        pos = g % q
        part = ff[la // q, (la % q) * tile:(la % q + 1) * tile, :].astype(bf16)

        @pl.when(owner == me)
        def _():
            fb[pos, c] = part

        @pl.when(owner != me)
        def _():
            fs[la] = part
            remote(fs.at[la], fb.at[pos, c], f_s.at[la], f_r.at[pos, c], (d, owner)).start()

    for pos in range(q):
        source = (me * q + pos) % R
        for cc in range(C):
            @pl.when((source != r) | (c != cc))
            def _():
                arrived(fb.at[pos, cc], f_r.at[pos, cc])
        total = fb[pos, 0].astype(f32)
        for cc in range(1, C):
            total = total + fb[pos, cc].astype(f32)
        out[pos * tile:(pos + 1) * tile, :] = total.astype(bf16)

    for h in range(2):
        for t in range(R):
            if t > 0:
                @pl.when(r < t)
                def _():
                    left(sup.at[h, t], up_s.at[h, t])
            if t < R - 1:
                @pl.when(r > t)
                def _():
                    left(sdn.at[h, t], dn_s.at[h, t])

            @pl.when((r >= t) & (r < R - 1))
            def _():
                left(gz.at[h, t], zu_s.at[h, t])

            @pl.when((r <= t) & (r > 0))
            def _():
                left(gz.at[h, t], zd_s.at[h, t])
        for k in range(1, C):
            left(gp.at[h, c], p_s.at[h, k])
    for t in range(R):
        @pl.when((r >= t) & (r < R - 1))
        def _():
            left(uz.at[t], wu_s.at[t])

        @pl.when((r <= t) & (r > 0))
        def _():
            left(uz.at[t], wd_s.at[t])
        for cc in range(C):
            left(ss.at[t, cc], c_s.at[t, cc])
    for k in range(1, C):
        cc = (c + k) % C
        left(ms.at[cc], m_s.at[cc])
    for la in range(tr):
        @pl.when((la * R + r) // q != me)
        def _():
            left(fs.at[la], f_s.at[la])


def grid_on_device(R, C, inputs, upstream, eig_tiles, eigvals):
    _, tr, tc, tile, _ = eig_tiles.shape
    tokens, width = inputs.shape
    slab = width // (R * C)
    q = slab // tile
    rows = tr * tile
    factor = 2.0 / (lax.axis_size("dp") * tokens)
    bf16, f32 = jnp.bfloat16, jnp.float32
    dma = pltpu.SemaphoreType.DMA
    piece = (tokens, slab)
    scratch = [
        pltpu.VMEM((R, rows, slab), bf16),
        pltpu.VMEM((2, tokens, rows), bf16),
        pltpu.VMEM((2, R) + piece, f32),
        pltpu.VMEM((2, R) + piece, bf16),
        pltpu.VMEM((2, R) + piece, bf16),
        pltpu.VMEM((2, R) + piece, bf16),
        pltpu.VMEM((2, R) + piece, bf16),
        pltpu.VMEM((2, R) + piece, bf16),
        pltpu.VMEM((2, C) + piece, bf16),
        pltpu.VMEM((R, C, slab, slab), f32),
        pltpu.VMEM((R, C, slab, slab), f32),
        pltpu.VMEM((R, C, slab, slab), bf16),
        pltpu.VMEM((R, C, slab, slab), bf16),
        pltpu.VMEM((C,) + piece, f32),
        pltpu.VMEM((C,) + piece, bf16),
        pltpu.VMEM((C,) + piece, bf16),
        pltpu.VMEM((R,) + piece, bf16),
        pltpu.VMEM((rows // slab, slab, tokens), f32),
        pltpu.VMEM((tr, tile, tokens), bf16),
        pltpu.VMEM((q, C, tile, tokens), bf16),
        dma((R,)), dma((2,)),
        dma((2, R)), dma((2, R)), dma((2, R)), dma((2, R)),
        dma((2, R)), dma((2, R)), dma((2, R)),
        dma((2, C)), dma((2, C)),
        dma((R, C)), dma((R, C)),
        dma((C,)), dma((C,)),
        dma((R,)), dma((R,)), dma((R,)),
        dma((tr,)), dma((q, C)),
    ]
    anywhere = pl.BlockSpec(memory_space=pl.ANY)
    return pl.pallas_call(
        functools.partial(line_kernel, (R, C, tr, tc, tile, slab, factor)),
        out_shape=jax.ShapeDtypeStruct((slab, tokens), bf16),
        in_specs=[pl.BlockSpec(memory_space=pltpu.VMEM), anywhere, anywhere, anywhere],
        out_specs=pl.BlockSpec(memory_space=pltpu.VMEM),
        scratch_shapes=scratch,
        compiler_params=pltpu.CompilerParams(
            collective_id=0, has_side_effects=True, vmem_limit_bytes=48 * 2**20
        ),
    )(eigvals.reshape(width // tile, tile), inputs, upstream, eig_tiles)


def body(inputs, upstream, eig_tiles, eigvals):
    width = inputs.shape[1]
    groups = lax.axis_size("mp")
    _, tr, tc, tile, _ = eig_tiles.shape
    R = width // (tr * tile)
    C = groups // R
    slab = width // groups
    whole_tiles = slab % tile == 0 and (tr * tile) % slab == 0 and tc % R == 0
    if lax.axis_size("dp") == 2 and whole_tiles and R > 1 and C > 1:
        return grid_on_device(R, C, inputs, upstream, eig_tiles, eigvals)
    return on_device(inputs, upstream, eig_tiles, eigvals)


def solution(mesh):
    return jax.shard_map(
        body,
        mesh=mesh,
        in_specs=(P("dp", None), P("dp", None), P("mp", None, None, None, None), P()),
        out_specs=P("mp", "dp"),
        check_vma=False,
    )
```

```python
import functools

import jax
import jax.numpy as jnp
from jax import lax
from jax.experimental import pallas as pl
from jax.experimental.pallas import tpu as pltpu
from jax.sharding import PartitionSpec as P


def kernel_of(left, right):
    root_left = jnp.sqrt(left)[:, None]
    root_right = jnp.sqrt(right)[None, :]
    return -1.0 / (root_left * root_right * (root_left + root_right))


def on_device(inputs, upstream, eig_tiles, eigvals):
    groups = lax.axis_size("mp")
    member = lax.axis_index("mp")
    width = eigvals.shape[0]
    slab = width // groups
    tile_rows = eig_tiles.shape[1]
    tile_cols = eig_tiles.shape[2]
    tile = eig_tiles.shape[3]
    grid_rows = width // (tile_rows * tile)
    grid_cols = groups // grid_rows
    piece = tile_cols * tile // groups
    local = jnp.transpose(eig_tiles[0], (0, 2, 1, 3)).reshape(tile_rows * tile, groups, piece)
    moved = lax.all_to_all(local, "mp", split_axis=1, concat_axis=1, tiled=True)
    moved = moved.reshape(tile_rows, tile, grid_rows, grid_cols, piece)
    basis = jnp.transpose(moved, (0, 2, 1, 3, 4)).reshape(width, slab)
    ordered = jnp.transpose(eigvals.reshape(tile_cols, grid_cols, tile), (1, 0, 2)).reshape(
        grid_cols, groups, piece
    )
    ordered = jnp.transpose(ordered, (1, 0, 2)).reshape(width)
    own = lax.dynamic_slice_in_dim(ordered, member * slab, slab)
    proj_in = jnp.dot(inputs, basis, preferred_element_type=jnp.float32).astype(jnp.bfloat16)
    proj_up = jnp.dot(upstream, basis, preferred_element_type=jnp.float32).astype(jnp.bfloat16)
    stacked = jnp.stack([proj_in, proj_up], 0)
    over_tokens = (((0,), (0,)), ((), ()))
    pieces = lax.all_gather(stacked, "mp", axis=2, tiled=True)
    part_in = pieces[0]
    part_up = pieces[1]
    block = lax.dot_general(proj_in, part_up, over_tokens, preferred_element_type=jnp.float32)
    block = block + lax.dot_general(
        proj_up, part_in, over_tokens, preferred_element_type=jnp.float32
    )
    joined = jnp.concatenate([block, part_in.astype(jnp.float32)], 0)
    gram = joined[:slab]
    all_in = joined[slab:].astype(jnp.bfloat16)
    total = lax.psum(gram.astype(jnp.bfloat16), "dp").astype(jnp.float32)
    weighted = (kernel_of(own, ordered) * (0.5 * total)).astype(jnp.bfloat16)
    over_columns = (((1,), (1,)), ((), ()))
    mixed = lax.dot_general(all_in, weighted, over_columns, preferred_element_type=jnp.float32)
    factor = 2.0 / (lax.axis_size("dp") * inputs.shape[0])
    update = (proj_up.astype(jnp.float32) / jnp.sqrt(own)[None, :] + factor * mixed).astype(
        jnp.bfloat16
    )
    own_rows = lax.all_to_all(basis, "mp", split_axis=0, concat_axis=1, tiled=True)
    every_update = lax.all_gather(update, "mp", axis=1, tiled=True)
    result = lax.dot_general(
        own_rows, every_update, over_columns, preferred_element_type=jnp.float32
    )
    return result.astype(jnp.bfloat16)


def line_kernel(
    dims, ev, x_in, x_up, eig, out,
    ub, xb, pf, sup, sdn, rup, rdn, gz, gp, kb, so, ss, sr, mx, ms, mr, uz, ff, fs, fa, fc, fb,
    ld_u, ld_x, up_s, up_r, dn_s, dn_r, zu_s, zd_s, z_r, p_s, p_r, c_s, c_r,
    m_s, m_r, wu_s, wd_s, w_r, f_s, f_r, o_s, o_r,
):
    R, C, tr, tc, tile, slab, tokens, parts, factor = dims
    q = slab // tile
    n = R * C
    rows = tr * tile
    d = lax.axis_index("dp")
    me = lax.axis_index("mp")
    r = me // C
    c = me % C
    partner = (1 - d, me)
    above = (d, (me + C) % n)
    below = (d, (me + n - C) % n)
    f32, bf16 = jnp.float32, jnp.bfloat16

    def span(i):
        return pl.ds(i * (tokens // parts), tokens // parts)

    def remote(src, dst, s_sem, r_sem, dev):
        return pltpu.make_async_remote_copy(
            src_ref=src, dst_ref=dst, send_sem=s_sem, recv_sem=r_sem,
            device_id=dev, device_id_type=pl.DeviceIdType.MESH,
        )

    def arrived(dst, r_sem):
        remote(dst, dst, c_s.at[0, 0], r_sem, partner).wait_recv()

    def left(src, s_sem):
        remote(src, src, s_sem, c_r.at[0, 0], partner).wait_send()

    for h, x in enumerate((x_in, x_up)):
        for la in range(tr):
            col = pl.multiple_of((la * R + r) * tile, tile)
            pltpu.make_async_copy(
                x.at[:, pl.ds(col, tile)], xb.at[h, :, la * tile:(la + 1) * tile], ld_x.at[h]
            ).start()
        if h == 0:
            for t in [R - 1, 0] + list(range(R - 2, 0, -1)):
                for k in range(q):
                    for la in range(tr):
                        pltpu.make_async_copy(
                            eig.at[0, la, t * q + k],
                            ub.at[t, la * tile:(la + 1) * tile, k * tile:(k + 1) * tile],
                            ld_u.at[t],
                        ).start()
    barrier = pltpu.get_barrier_semaphore()
    for k in range(1, n):
        pl.semaphore_signal(
            barrier, inc=1, device_id=(d, (me + k) % n), device_id_type=pl.DeviceIdType.MESH
        )
    pl.semaphore_signal(
        barrier, inc=1, device_id=partner, device_id_type=pl.DeviceIdType.MESH
    )
    pl.semaphore_wait(barrier, n)

    for h in range(2):
        pltpu.make_async_copy(xb.at[h], xb.at[h], ld_x.at[h]).wait()
        for t in [R - 1, 0] + list(range(R - 2, 0, -1)):
            if h == 0:
                pltpu.make_async_copy(ub.at[t], ub.at[t], ld_u.at[t]).wait()
            pf[h, t] = jnp.dot(xb[h], ub[t], preferred_element_type=f32)
            if t > 0:
                @pl.when(r == 0)
                def _():
                    sup[h, t] = pf[h, t].astype(bf16)
                    remote(sup.at[h, t], rup.at[h, t], up_s.at[h, t], up_r.at[h, t], above).start()
            if t < R - 1:
                @pl.when(r == R - 1)
                def _():
                    sdn[h, t] = pf[h, t].astype(bf16)
                    remote(sdn.at[h, t], rdn.at[h, t], dn_s.at[h, t], dn_r.at[h, t], below).start()

    def kernel_rows(lb, carry):
        row = jnp.sqrt(ev[pl.ds(lb * C + c, 1), :])
        sj = jnp.broadcast_to(row, (tile, tile)).T
        t = lb // q
        at = pl.multiple_of((lb % q) * tile, tile)
        for cc in range(C):
            for k in range(q):
                si = jnp.sqrt(ev[pl.ds((r * q + k) * C + cc, 1), :])
                kb[t, cc, pl.ds(at, tile), k * tile:(k + 1) * tile] = -0.5 / (si * sj * (si + sj))
        return carry

    lax.fori_loop(0, tc, kernel_rows, 0)

    def relay_up(h):
        for t in range(R - 1, 0, -1):
            @pl.when((r > 0) & (r < t))
            def _():
                arrived(rup.at[h, t], up_r.at[h, t])
                sup[h, t] = (pf[h, t] + rup[h, t].astype(f32)).astype(bf16)
                remote(sup.at[h, t], rup.at[h, t], up_s.at[h, t], up_r.at[h, t], above).start()

    def relay_down(h):
        for t in range(R - 1):
            @pl.when((r < R - 1) & (r > t))
            def _():
                arrived(rdn.at[h, t], dn_r.at[h, t])
                sdn[h, t] = (pf[h, t] + rdn[h, t].astype(f32)).astype(bf16)
                remote(sdn.at[h, t], rdn.at[h, t], dn_s.at[h, t], dn_r.at[h, t], below).start()

    for h in range(2):
        @pl.when(r < R // 2)
        def _():
            relay_up(h)
            relay_down(h)

        @pl.when(r >= R // 2)
        def _():
            relay_down(h)
            relay_up(h)

        for t in range(R):
            @pl.when(r == t)
            def _():
                total = pf[h, t]
                if t > 0:
                    arrived(rup.at[h, t], up_r.at[h, t])
                    total = total + rup[h, t].astype(f32)
                if t < R - 1:
                    arrived(rdn.at[h, t], dn_r.at[h, t])
                    total = total + rdn[h, t].astype(f32)
                total = total.astype(bf16)
                gz[h, t] = total
                for i in range(parts):
                    buf = gz.at[h, t, span(i)]
                    if t < R - 1:
                        remote(buf, buf, zu_s.at[h, i, t], z_r.at[h, i, t], above).start()
                    if t > 0:
                        remote(buf, buf, zd_s.at[h, i, t], z_r.at[h, i, t], below).start()
                gp[h, c] = total
        for k in range(1, C):
            cc = (c + k) % C
            remote(
                gp.at[h, c], gp.at[h, c], p_s.at[h, k], p_r.at[h, c], (d, r * C + cc)
            ).start()

    def each_piece(body):
        body(r, None)
        for k in range(1, R):
            @pl.when(r >= k)
            def _():
                body(r - k, True)

            @pl.when(r + k < R)
            def _():
                body(r + k, False)

    def relay(buf, s, from_below, s_up, s_dn, r_sem):
        arrived(buf, r_sem)
        if from_below:
            @pl.when(r < R - 1)
            def _():
                remote(buf, buf, s_up, r_sem, above).start()
        else:
            @pl.when(r > 0)
            def _():
                remote(buf, buf, s_dn, r_sem, below).start()

    tokens_both = (((0,), (0,)), ((), ()))
    mx[...] = jnp.zeros_like(mx)

    def mixed_block(s, cc, carry):
        arrived(sr.at[s, cc], c_r.at[s, cc])
        weighted = (kb[s, cc] * (so[s, cc] + sr[s, cc].astype(f32))).astype(bf16)
        mx[cc] += jnp.dot(gz[0, s], weighted, preferred_element_type=f32)
        return carry

    def gram_piece(s, from_below):
        if from_below is not None:
            for h in range(2):
                for i in range(parts):
                    relay(
                        gz.at[h, s, span(i)], s, from_below,
                        zu_s.at[h, i, s], zd_s.at[h, i, s], z_r.at[h, i, s],
                    )

        def one(cc, carry):
            block = lax.dot_general(gz[1, s], gp[0, cc], tokens_both, preferred_element_type=f32)
            block = block + lax.dot_general(
                gz[0, s], gp[1, cc], tokens_both, preferred_element_type=f32
            )
            so[s, cc] = block
            ss[s, cc] = block.astype(bf16)
            remote(ss.at[s, cc], sr.at[s, cc], c_s.at[s, cc], c_r.at[s, cc], partner).start()
            return carry

        lax.fori_loop(0, C, one, 0)
        lax.fori_loop(0, C, functools.partial(mixed_block, s), 0)

    for h in range(2):
        for k in range(1, C):
            cc = (c + k) % C
            arrived(gp.at[h, cc], p_r.at[h, cc])
    each_piece(gram_piece)

    for k in range(1, C):
        cc = (c + k) % C
        ms[cc] = mx[cc].astype(bf16)
        remote(ms.at[cc], mr.at[c], m_s.at[cc], m_r.at[c], (d, r * C + cc)).start()
    total = mx[c]
    for k in range(1, C):
        cc = (c + k) % C
        arrived(mr.at[cc], m_r.at[cc])
        total = total + mr[cc].astype(f32)
    roots = jnp.concatenate(
        [jnp.sqrt(ev[pl.ds((r * q + k) * C + c, 1), :]) for k in range(q)], axis=1
    )
    uz[r] = (gz[1, r].astype(f32) / roots + factor * total).astype(bf16)

    for i in range(parts):
        buf = uz.at[r, span(i)]

        @pl.when(r < R - 1)
        def _():
            remote(buf, buf, wu_s.at[i, r], w_r.at[i, r], above).start()

        @pl.when(r > 0)
        def _():
            remote(buf, buf, wd_s.at[i, r], w_r.at[i, r], below).start()

    ff[...] = jnp.zeros_like(ff)
    chunks = rows // slab

    def grad_piece(s, from_below):
        if from_below is not None:
            for i in range(parts):
                relay(
                    uz.at[s, span(i)], s, from_below, wu_s.at[i, s], wd_s.at[i, s], w_r.at[i, s]
                )

        def one(i, carry):
            at = pl.multiple_of(i * slab, slab)
            ff[i] += lax.dot_general(
                ub[s, pl.ds(at, slab), :], uz[s], (((1,), (1,)), ((), ())),
                preferred_element_type=f32,
            )
            return carry

        lax.fori_loop(0, chunks, one, 0)

    each_piece(grad_piece)

    half = C // 2
    for la in range(tr):
        place = (la % 2) * half + (la // 2) % half
        fs[la] = ff[la // q, (la % q) * tile:(la % q + 1) * tile, :].astype(bf16)

        @pl.when(c != place)
        def _():
            remote(
                fs.at[la], fa.at[la // C, c], f_s.at[la], f_r.at[la // C, c], (d, r * C + place)
            ).start()

    for j in range(tr // C):
        la = c // half + 2 * (c % half) + C * j
        total = fs[la].astype(f32)
        for k in range(1, C):
            cc = (c + k) % C
            arrived(fa.at[j, cc], f_r.at[j, cc])
            total = total + fa[j, cc].astype(f32)
        owner = (la * R + r) // q
        pos = (la * R + r) % q
        fc[j] = total.astype(bf16)

        @pl.when(owner == me)
        def _():
            fb[pos] = fc[j]

        @pl.when(owner != me)
        def _():
            remote(fc.at[j], fb.at[pos], o_s.at[j], o_r.at[pos], (d, owner)).start()

    for pos in range(q):
        g = me * q + pos
        la = g // R
        place = (la % 2) * half + (la // 2) % half

        @pl.when((g % R) * C + place != me)
        def _():
            arrived(fb.at[pos], o_r.at[pos])

        out[pos * tile:(pos + 1) * tile, :] = fb[pos]

    for h in range(2):
        for t in range(R):
            if t > 0:
                @pl.when(r < t)
                def _():
                    left(sup.at[h, t], up_s.at[h, t])
            if t < R - 1:
                @pl.when(r > t)
                def _():
                    left(sdn.at[h, t], dn_s.at[h, t])

            for i in range(parts):
                @pl.when((r >= t) & (r < R - 1))
                def _():
                    left(gz.at[h, t, span(i)], zu_s.at[h, i, t])

                @pl.when((r <= t) & (r > 0))
                def _():
                    left(gz.at[h, t, span(i)], zd_s.at[h, i, t])
        for k in range(1, C):
            left(gp.at[h, c], p_s.at[h, k])
    for t in range(R):
        for i in range(parts):
            @pl.when((r >= t) & (r < R - 1))
            def _():
                left(uz.at[t, span(i)], wu_s.at[i, t])

            @pl.when((r <= t) & (r > 0))
            def _():
                left(uz.at[t, span(i)], wd_s.at[i, t])
        for cc in range(C):
            left(ss.at[t, cc], c_s.at[t, cc])
    for k in range(1, C):
        cc = (c + k) % C
        left(ms.at[cc], m_s.at[cc])
    for la in range(tr):
        @pl.when(c != (la % 2) * half + (la // 2) % half)
        def _():
            left(fs.at[la], f_s.at[la])
    for j in range(tr // C):
        la = c // half + 2 * (c % half) + C * j

        @pl.when((la * R + r) // q != me)
        def _():
            left(fc.at[j], o_s.at[j])


def grid_on_device(R, C, inputs, upstream, eig_tiles, eigvals):
    _, tr, tc, tile, _ = eig_tiles.shape
    tokens, width = inputs.shape
    slab = width // (R * C)
    q = slab // tile
    parts = 2 if tokens % 32 == 0 else 1
    rows = tr * tile
    factor = 2.0 / (lax.axis_size("dp") * tokens)
    bf16, f32 = jnp.bfloat16, jnp.float32
    dma = pltpu.SemaphoreType.DMA
    piece = (tokens, slab)
    scratch = [
        pltpu.VMEM((R, rows, slab), bf16),
        pltpu.VMEM((2, tokens, rows), bf16),
        pltpu.VMEM((2, R) + piece, f32),
        pltpu.VMEM((2, R) + piece, bf16),
        pltpu.VMEM((2, R) + piece, bf16),
        pltpu.VMEM((2, R) + piece, bf16),
        pltpu.VMEM((2, R) + piece, bf16),
        pltpu.VMEM((2, R) + piece, bf16),
        pltpu.VMEM((2, C) + piece, bf16),
        pltpu.VMEM((R, C, slab, slab), f32),
        pltpu.VMEM((R, C, slab, slab), f32),
        pltpu.VMEM((R, C, slab, slab), bf16),
        pltpu.VMEM((R, C, slab, slab), bf16),
        pltpu.VMEM((C,) + piece, f32),
        pltpu.VMEM((C,) + piece, bf16),
        pltpu.VMEM((C,) + piece, bf16),
        pltpu.VMEM((R,) + piece, bf16),
        pltpu.VMEM((rows // slab, slab, tokens), f32),
        pltpu.VMEM((tr, tile, tokens), bf16),
        pltpu.VMEM((tr // C, C, tile, tokens), bf16),
        pltpu.VMEM((tr // C, tile, tokens), bf16),
        pltpu.VMEM((q, tile, tokens), bf16),
        dma((R,)), dma((2,)),
        dma((2, R)), dma((2, R)), dma((2, R)), dma((2, R)),
        dma((2, parts, R)), dma((2, parts, R)), dma((2, parts, R)),
        dma((2, C)), dma((2, C)),
        dma((R, C)), dma((R, C)),
        dma((C,)), dma((C,)),
        dma((parts, R)), dma((parts, R)), dma((parts, R)),
        dma((tr,)), dma((tr // C, C)), dma((tr // C,)), dma((q,)),
    ]
    anywhere = pl.BlockSpec(memory_space=pltpu.HBM)
    return pl.pallas_call(
        functools.partial(line_kernel, (R, C, tr, tc, tile, slab, tokens, parts, factor)),
        out_shape=jax.ShapeDtypeStruct((slab, tokens), bf16),
        in_specs=[pl.BlockSpec(memory_space=pltpu.VMEM), anywhere, anywhere, anywhere],
        out_specs=pl.BlockSpec(memory_space=pltpu.VMEM),
        scratch_shapes=scratch,
        compiler_params=pltpu.CompilerParams(
            collective_id=0, has_side_effects=True, vmem_limit_bytes=67_043_328
        ),
    )(eigvals.reshape(width // tile, tile), inputs, upstream, eig_tiles)


def body(inputs, upstream, eig_tiles, eigvals):
    width = inputs.shape[1]
    groups = lax.axis_size("mp")
    _, tr, tc, tile, _ = eig_tiles.shape
    R = width // (tr * tile)
    C = groups // R
    slab = width // groups
    whole_tiles = slab % tile == 0 and (tr * tile) % slab == 0 and tc % R == 0
    if lax.axis_size("dp") == 2 and whole_tiles and R > 1 and C % 2 == 0 and tr % C == 0:
        return grid_on_device(R, C, inputs, upstream, eig_tiles, eigvals)
    return on_device(inputs, upstream, eig_tiles, eigvals)


def solution(mesh):
    return jax.shard_map(
        body,
        mesh=mesh,
        in_specs=(P("dp", None), P("dp", None), P("mp", None, None, None, None), P()),
        out_specs=P("mp", "dp"),
        check_vma=False,
    )
```

```python
import functools

import jax
import jax.numpy as jnp
from jax import lax
from jax.experimental import pallas as pl
from jax.experimental.pallas import tpu as pltpu
from jax.sharding import PartitionSpec as P


def kernel_of(left, right):
    root_left = jnp.sqrt(left)[:, None]
    root_right = jnp.sqrt(right)[None, :]
    return -1.0 / (root_left * root_right * (root_left + root_right))


def on_device(inputs, upstream, eig_tiles, eigvals):
    groups = lax.axis_size("mp")
    member = lax.axis_index("mp")
    width = eigvals.shape[0]
    slab = width // groups
    tile_rows = eig_tiles.shape[1]
    tile_cols = eig_tiles.shape[2]
    tile = eig_tiles.shape[3]
    grid_rows = width // (tile_rows * tile)
    grid_cols = groups // grid_rows
    piece = tile_cols * tile // groups
    local = jnp.transpose(eig_tiles[0], (0, 2, 1, 3)).reshape(tile_rows * tile, groups, piece)
    moved = lax.all_to_all(local, "mp", split_axis=1, concat_axis=1, tiled=True)
    moved = moved.reshape(tile_rows, tile, grid_rows, grid_cols, piece)
    basis = jnp.transpose(moved, (0, 2, 1, 3, 4)).reshape(width, slab)
    ordered = jnp.transpose(eigvals.reshape(tile_cols, grid_cols, tile), (1, 0, 2)).reshape(
        grid_cols, groups, piece
    )
    ordered = jnp.transpose(ordered, (1, 0, 2)).reshape(width)
    own = lax.dynamic_slice_in_dim(ordered, member * slab, slab)
    proj_in = jnp.dot(inputs, basis, preferred_element_type=jnp.float32).astype(jnp.bfloat16)
    proj_up = jnp.dot(upstream, basis, preferred_element_type=jnp.float32).astype(jnp.bfloat16)
    stacked = jnp.stack([proj_in, proj_up], 0)
    over_tokens = (((0,), (0,)), ((), ()))
    pieces = lax.all_gather(stacked, "mp", axis=2, tiled=True)
    part_in = pieces[0]
    part_up = pieces[1]
    block = lax.dot_general(proj_in, part_up, over_tokens, preferred_element_type=jnp.float32)
    block = block + lax.dot_general(
        proj_up, part_in, over_tokens, preferred_element_type=jnp.float32
    )
    joined = jnp.concatenate([block, part_in.astype(jnp.float32)], 0)
    gram = joined[:slab]
    all_in = joined[slab:].astype(jnp.bfloat16)
    total = lax.psum(gram.astype(jnp.bfloat16), "dp").astype(jnp.float32)
    weighted = (kernel_of(own, ordered) * (0.5 * total)).astype(jnp.bfloat16)
    over_columns = (((1,), (1,)), ((), ()))
    mixed = lax.dot_general(all_in, weighted, over_columns, preferred_element_type=jnp.float32)
    factor = 2.0 / (lax.axis_size("dp") * inputs.shape[0])
    update = (proj_up.astype(jnp.float32) / jnp.sqrt(own)[None, :] + factor * mixed).astype(
        jnp.bfloat16
    )
    own_rows = lax.all_to_all(basis, "mp", split_axis=0, concat_axis=1, tiled=True)
    every_update = lax.all_gather(update, "mp", axis=1, tiled=True)
    result = lax.dot_general(
        own_rows, every_update, over_columns, preferred_element_type=jnp.float32
    )
    return result.astype(jnp.bfloat16)


def line_kernel(
    dims, ev, x_in, x_up, eig, out,
    ub, xb, pf, sup, sdn, rup, rdn, gz, gp, kb, so, ss, sr, zt, mx, ms, mr, uz, ff, fs, fa, fc, fb,
    ld_u, ld_x, up_s, up_r, dn_s, dn_r, zu_s, zd_s, z_r, p_s, p_r, c_s, c_r,
    m_s, m_r, wu_s, wd_s, w_r, f_s, f_r, o_s, o_r,
):
    R, C, tr, tc, tile, slab, tokens, parts, factor = dims
    q = slab // tile
    n = R * C
    rows = tr * tile
    d = lax.axis_index("dp")
    me = lax.axis_index("mp")
    r = me // C
    c = me % C
    partner = (1 - d, me)
    above = (d, (me + C) % n)
    below = (d, (me + n - C) % n)
    f32, bf16 = jnp.float32, jnp.bfloat16

    def span(i):
        return pl.ds(i * (tokens // parts), tokens // parts)

    def remote(src, dst, s_sem, r_sem, dev):
        return pltpu.make_async_remote_copy(
            src_ref=src, dst_ref=dst, send_sem=s_sem, recv_sem=r_sem,
            device_id=dev, device_id_type=pl.DeviceIdType.MESH,
        )

    def arrived(dst, r_sem):
        remote(dst, dst, c_s.at[0, 0], r_sem, partner).wait_recv()

    def left(src, s_sem):
        remote(src, src, s_sem, c_r.at[0, 0], partner).wait_send()

    barrier = pltpu.get_barrier_semaphore()
    for k in range(1, n):
        pl.semaphore_signal(
            barrier, inc=1, device_id=(d, (me + k) % n), device_id_type=pl.DeviceIdType.MESH
        )
    pl.semaphore_signal(
        barrier, inc=1, device_id=partner, device_id_type=pl.DeviceIdType.MESH
    )
    order = [R - 1, 0] + list(range(R - 2, 0, -1))
    for h, x in enumerate((x_in, x_up)):
        for la in range(tr):
            col = pl.multiple_of((la * R + r) * tile, tile)
            pltpu.make_async_copy(
                x.at[:, pl.ds(col, tile)], xb.at[h, :, la * tile:(la + 1) * tile], ld_x.at[h]
            ).start()
        if h == 0:
            for t in order:
                for k in range(q):
                    pltpu.make_async_copy(
                        eig.at[0, :, t * q + k],
                        ub.at[t, :, :, k * tile:(k + 1) * tile],
                        ld_u.at[t],
                    ).start()

    for h in range(2):
        pltpu.make_async_copy(xb.at[h], xb.at[h], ld_x.at[h]).wait()
        for t in order:
            if h == 0:
                pltpu.make_async_copy(ub.at[t], ub.at[t], ld_u.at[t]).wait()
            pf[h, t] = jnp.dot(
                xb[h], ub[t].reshape(rows, slab), preferred_element_type=f32
            )
            if h == 0 and t == order[0]:
                pl.semaphore_wait(barrier, n)
            if t > 0:
                @pl.when(r == 0)
                def _():
                    sup[h, t] = pf[h, t].astype(bf16)
                    remote(sup.at[h, t], rup.at[h, t], up_s.at[h, t], up_r.at[h, t], above).start()
            if t < R - 1:
                @pl.when(r == R - 1)
                def _():
                    sdn[h, t] = pf[h, t].astype(bf16)
                    remote(sdn.at[h, t], rdn.at[h, t], dn_s.at[h, t], dn_r.at[h, t], below).start()

    def relay_up(h):
        for t in range(R - 1, 0, -1):
            @pl.when((r > 0) & (r < t))
            def _():
                arrived(rup.at[h, t], up_r.at[h, t])
                sup[h, t] = (pf[h, t] + rup[h, t].astype(f32)).astype(bf16)
                remote(sup.at[h, t], rup.at[h, t], up_s.at[h, t], up_r.at[h, t], above).start()

    def relay_down(h):
        for t in range(R - 1):
            @pl.when((r < R - 1) & (r > t))
            def _():
                arrived(rdn.at[h, t], dn_r.at[h, t])
                sdn[h, t] = (pf[h, t] + rdn[h, t].astype(f32)).astype(bf16)
                remote(sdn.at[h, t], rdn.at[h, t], dn_s.at[h, t], dn_r.at[h, t], below).start()

    for h in range(2):
        @pl.when(r < R // 2)
        def _():
            relay_up(h)
            relay_down(h)

        @pl.when(r >= R // 2)
        def _():
            relay_down(h)
            relay_up(h)

        for t in range(R):
            @pl.when(r == t)
            def _():
                total = pf[h, t]
                if t > 0:
                    arrived(rup.at[h, t], up_r.at[h, t])
                    total = total + rup[h, t].astype(f32)
                if t < R - 1:
                    arrived(rdn.at[h, t], dn_r.at[h, t])
                    total = total + rdn[h, t].astype(f32)
                total = total.astype(bf16)
                gz[h, t] = total
                for i in range(parts):
                    buf = gz.at[h, t, span(i)]
                    if t < R - 1:
                        remote(buf, buf, zu_s.at[h, i, t], z_r.at[h, i, t], above).start()
                    if t > 0:
                        remote(buf, buf, zd_s.at[h, i, t], z_r.at[h, i, t], below).start()
                gp[h, c] = total
        for k in range(1, C):
            cc = (c + k) % C
            remote(
                gp.at[h, c], gp.at[h, c], p_s.at[h, k], p_r.at[h, c], (d, r * C + cc)
            ).start()

    def kernel_rows(lb, carry):
        row = jnp.sqrt(ev[pl.ds(lb * C + c, 1), :])
        sj = jnp.broadcast_to(row, (tile, tile)).T
        t = lb // q
        at = pl.multiple_of((lb % q) * tile, tile)
        for cc in range(C):
            for k in range(q):
                si = jnp.sqrt(ev[pl.ds((r * q + k) * C + cc, 1), :])
                kb[t, cc, pl.ds(at, tile), k * tile:(k + 1) * tile] = -0.5 / (si * sj * (si + sj))
        return carry

    lax.fori_loop(0, tc, kernel_rows, 0)

    def level(k, body):
        if k == 0:
            body(r, None)
        elif k < R:
            @pl.when(r >= k)
            def _():
                body(r - k, True)

            @pl.when(r + k < R)
            def _():
                body(r + k, False)

    def relay(buf, s, from_below, s_up, s_dn, r_sem):
        arrived(buf, r_sem)
        if from_below:
            @pl.when(r < R - 1)
            def _():
                remote(buf, buf, s_up, r_sem, above).start()
        else:
            @pl.when(r > 0)
            def _():
                remote(buf, buf, s_dn, r_sem, below).start()

    mx[...] = jnp.zeros_like(mx)

    def mixed_block(s, cc, carry):
        arrived(sr.at[s, cc], c_r.at[s, cc])
        weighted = (kb[s, cc] * (so[s, cc] + sr[s, cc].astype(f32))).astype(bf16)
        mx[cc] += jnp.dot(gz[0, s], weighted, preferred_element_type=f32)
        return carry

    def relay_piece(s, from_below):
        for h in range(2):
            for i in range(parts):
                relay(
                    gz.at[h, s, span(i)], s, from_below,
                    zu_s.at[h, i, s], zd_s.at[h, i, s], z_r.at[h, i, s],
                )

    def gram_piece(s, from_below):
        for h in range(2):
            zt[h] = gz[h, s].T

        def one(cc, carry):
            block = jnp.dot(zt[1], gp[0, cc], preferred_element_type=f32)
            block = block + jnp.dot(zt[0], gp[1, cc], preferred_element_type=f32)
            so[s, cc] = block
            ss[s, cc] = block.astype(bf16)
            remote(ss.at[s, cc], sr.at[s, cc], c_s.at[s, cc], c_r.at[s, cc], partner).start()
            return carry

        lax.fori_loop(0, C, one, 0)

    def mixed_piece(s, from_below):
        lax.fori_loop(0, C, functools.partial(mixed_block, s), 0)

    level(1, relay_piece)
    for h in range(2):
        for k in range(1, C):
            cc = (c + k) % C
            arrived(gp.at[h, cc], p_r.at[h, cc])
    for k in range(R):
        level(k, gram_piece)
        if k + 2 < R:
            level(k + 2, relay_piece)
        if k > 0:
            level(k - 1, mixed_piece)
    level(R - 1, mixed_piece)

    for i in range(parts):
        for k in range(1, C):
            cc = (c + k) % C
            ms[cc, span(i)] = mx[cc, span(i)].astype(bf16)
            remote(
                ms.at[cc, span(i)], mr.at[c, span(i)], m_s.at[i, cc], m_r.at[i, c],
                (d, r * C + cc),
            ).start()
    roots = jnp.concatenate(
        [jnp.sqrt(ev[pl.ds((r * q + k) * C + c, 1), :]) for k in range(q)], axis=1
    )
    for i in range(parts):
        total = mx[c, span(i)]
        for k in range(1, C):
            cc = (c + k) % C
            arrived(mr.at[cc, span(i)], m_r.at[i, cc])
            total = total + mr[cc, span(i)].astype(f32)
        uz[r, span(i)] = (gz[1, r, span(i)].astype(f32) / roots + factor * total).astype(bf16)
        buf = uz.at[r, span(i)]

        @pl.when(r < R - 1)
        def _():
            remote(buf, buf, wu_s.at[i, r], w_r.at[i, r], above).start()

        @pl.when(r > 0)
        def _():
            remote(buf, buf, wd_s.at[i, r], w_r.at[i, r], below).start()

    ff[...] = jnp.zeros_like(ff)
    chunks = rows // slab

    def relay_update(s, from_below):
        for i in range(parts):
            relay(
                uz.at[s, span(i)], s, from_below, wu_s.at[i, s], wd_s.at[i, s], w_r.at[i, s]
            )

    def grad_piece(s, from_below):
        def one(i, carry):
            ff[i] += lax.dot_general(
                ub[s, pl.ds(i * q, q)].reshape(slab, slab), uz[s], (((1,), (1,)), ((), ())),
                preferred_element_type=f32,
            )
            return carry

        lax.fori_loop(0, chunks, one, 0)

    for k in range(R):
        level(k, grad_piece)
        if k == 0:
            level(1, relay_update)
        level(k + 2, relay_update)

    half = C // 2
    for la in range(tr):
        place = (la % 2) * half + (la // 2) % half
        fs[la] = ff[la // q, (la % q) * tile:(la % q + 1) * tile, :].astype(bf16)

        @pl.when(c != place)
        def _():
            remote(
                fs.at[la], fa.at[la // C, c], f_s.at[la], f_r.at[la // C, c], (d, r * C + place)
            ).start()

    for j in range(tr // C):
        la = c // half + 2 * (c % half) + C * j
        total = fs[la].astype(f32)
        for k in range(1, C):
            cc = (c + k) % C
            arrived(fa.at[j, cc], f_r.at[j, cc])
            total = total + fa[j, cc].astype(f32)
        owner = (la * R + r) // q
        pos = (la * R + r) % q
        fc[j] = total.astype(bf16)

        @pl.when(owner == me)
        def _():
            fb[pos] = fc[j]

        @pl.when(owner != me)
        def _():
            remote(fc.at[j], fb.at[pos], o_s.at[j], o_r.at[pos], (d, owner)).start()

    for pos in range(q):
        g = me * q + pos
        la = g // R
        place = (la % 2) * half + (la // 2) % half

        @pl.when((g % R) * C + place != me)
        def _():
            arrived(fb.at[pos], o_r.at[pos])

        out[pos * tile:(pos + 1) * tile, :] = fb[pos]

    for h in range(2):
        for t in range(R):
            if t > 0:
                @pl.when(r < t)
                def _():
                    left(sup.at[h, t], up_s.at[h, t])
            if t < R - 1:
                @pl.when(r > t)
                def _():
                    left(sdn.at[h, t], dn_s.at[h, t])

            for i in range(parts):
                @pl.when((r >= t) & (r < R - 1))
                def _():
                    left(gz.at[h, t, span(i)], zu_s.at[h, i, t])

                @pl.when((r <= t) & (r > 0))
                def _():
                    left(gz.at[h, t, span(i)], zd_s.at[h, i, t])
        for k in range(1, C):
            left(gp.at[h, c], p_s.at[h, k])
    for t in range(R):
        for i in range(parts):
            @pl.when((r >= t) & (r < R - 1))
            def _():
                left(uz.at[t, span(i)], wu_s.at[i, t])

            @pl.when((r <= t) & (r > 0))
            def _():
                left(uz.at[t, span(i)], wd_s.at[i, t])
        for cc in range(C):
            left(ss.at[t, cc], c_s.at[t, cc])
    for k in range(1, C):
        cc = (c + k) % C
        for i in range(parts):
            left(ms.at[cc, span(i)], m_s.at[i, cc])
    for la in range(tr):
        @pl.when(c != (la % 2) * half + (la // 2) % half)
        def _():
            left(fs.at[la], f_s.at[la])
    for j in range(tr // C):
        la = c // half + 2 * (c % half) + C * j

        @pl.when((la * R + r) // q != me)
        def _():
            left(fc.at[j], o_s.at[j])


def grid_on_device(R, C, inputs, upstream, eig_tiles, eigvals):
    _, tr, tc, tile, _ = eig_tiles.shape
    tokens, width = inputs.shape
    slab = width // (R * C)
    q = slab // tile
    parts = 2 if tokens % 32 == 0 else 1
    rows = tr * tile
    factor = 2.0 / (lax.axis_size("dp") * tokens)
    bf16, f32 = jnp.bfloat16, jnp.float32
    dma = pltpu.SemaphoreType.DMA
    piece = (tokens, slab)
    scratch = [
        pltpu.VMEM((R, tr, tile, slab), bf16),
        pltpu.VMEM((2, tokens, rows), bf16),
        pltpu.VMEM((2, R) + piece, f32),
        pltpu.VMEM((2, R) + piece, bf16),
        pltpu.VMEM((2, R) + piece, bf16),
        pltpu.VMEM((2, R) + piece, bf16),
        pltpu.VMEM((2, R) + piece, bf16),
        pltpu.VMEM((2, R) + piece, bf16),
        pltpu.VMEM((2, C) + piece, bf16),
        pltpu.VMEM((R, C, slab, slab), f32),
        pltpu.VMEM((R, C, slab, slab), f32),
        pltpu.VMEM((R, C, slab, slab), bf16),
        pltpu.VMEM((R, C, slab, slab), bf16),
        pltpu.VMEM((2, slab, tokens), bf16),
        pltpu.VMEM((C,) + piece, f32),
        pltpu.VMEM((C,) + piece, bf16),
        pltpu.VMEM((C,) + piece, bf16),
        pltpu.VMEM((R,) + piece, bf16),
        pltpu.VMEM((rows // slab, slab, tokens), f32),
        pltpu.VMEM((tr, tile, tokens), bf16),
        pltpu.VMEM((tr // C, C, tile, tokens), bf16),
        pltpu.VMEM((tr // C, tile, tokens), bf16),
        pltpu.VMEM((q, tile, tokens), bf16),
        dma((R,)), dma((2,)),
        dma((2, R)), dma((2, R)), dma((2, R)), dma((2, R)),
        dma((2, parts, R)), dma((2, parts, R)), dma((2, parts, R)),
        dma((2, C)), dma((2, C)),
        dma((R, C)), dma((R, C)),
        dma((parts, C)), dma((parts, C)),
        dma((parts, R)), dma((parts, R)), dma((parts, R)),
        dma((tr,)), dma((tr // C, C)), dma((tr // C,)), dma((q,)),
    ]
    anywhere = pl.BlockSpec(memory_space=pltpu.HBM)
    return pl.pallas_call(
        functools.partial(line_kernel, (R, C, tr, tc, tile, slab, tokens, parts, factor)),
        out_shape=jax.ShapeDtypeStruct((slab, tokens), bf16),
        in_specs=[pl.BlockSpec(memory_space=pltpu.VMEM), anywhere, anywhere, anywhere],
        out_specs=pl.BlockSpec(memory_space=pltpu.VMEM),
        scratch_shapes=scratch,
        compiler_params=pltpu.CompilerParams(
            collective_id=0, has_side_effects=True, vmem_limit_bytes=65_800_000
        ),
    )(eigvals.reshape(width // tile, tile), inputs, upstream, eig_tiles)


def body(inputs, upstream, eig_tiles, eigvals):
    width = inputs.shape[1]
    groups = lax.axis_size("mp")
    _, tr, tc, tile, _ = eig_tiles.shape
    R = width // (tr * tile)
    C = groups // R
    slab = width // groups
    whole_tiles = slab % tile == 0 and (tr * tile) % slab == 0 and tc % R == 0
    if lax.axis_size("dp") == 2 and whole_tiles and R > 1 and C % 2 == 0 and tr % C == 0:
        return grid_on_device(R, C, inputs, upstream, eig_tiles, eigvals)
    return on_device(inputs, upstream, eig_tiles, eigvals)


def solution(mesh):
    return jax.shard_map(
        body,
        mesh=mesh,
        in_specs=(P("dp", None), P("dp", None), P("mp", None, None, None, None), P()),
        out_specs=P("mp", "dp"),
        check_vma=False,
    )
```

```python
import functools

import jax
import jax.numpy as jnp
from jax import lax
from jax.experimental import pallas as pl
from jax.experimental.pallas import tpu as pltpu
from jax.sharding import PartitionSpec as P


def kernel_of(left, right):
    root_left = jnp.sqrt(left)[:, None]
    root_right = jnp.sqrt(right)[None, :]
    return -1.0 / (root_left * root_right * (root_left + root_right))


def on_device(inputs, upstream, eig_tiles, eigvals):
    groups = lax.axis_size("mp")
    member = lax.axis_index("mp")
    width = eigvals.shape[0]
    slab = width // groups
    tile_rows = eig_tiles.shape[1]
    tile_cols = eig_tiles.shape[2]
    tile = eig_tiles.shape[3]
    grid_rows = width // (tile_rows * tile)
    grid_cols = groups // grid_rows
    piece = tile_cols * tile // groups
    local = jnp.transpose(eig_tiles[0], (0, 2, 1, 3)).reshape(tile_rows * tile, groups, piece)
    moved = lax.all_to_all(local, "mp", split_axis=1, concat_axis=1, tiled=True)
    moved = moved.reshape(tile_rows, tile, grid_rows, grid_cols, piece)
    basis = jnp.transpose(moved, (0, 2, 1, 3, 4)).reshape(width, slab)
    ordered = jnp.transpose(eigvals.reshape(tile_cols, grid_cols, tile), (1, 0, 2)).reshape(
        grid_cols, groups, piece
    )
    ordered = jnp.transpose(ordered, (1, 0, 2)).reshape(width)
    own = lax.dynamic_slice_in_dim(ordered, member * slab, slab)
    proj_in = jnp.dot(inputs, basis, preferred_element_type=jnp.float32).astype(jnp.bfloat16)
    proj_up = jnp.dot(upstream, basis, preferred_element_type=jnp.float32).astype(jnp.bfloat16)
    stacked = jnp.stack([proj_in, proj_up], 0)
    over_tokens = (((0,), (0,)), ((), ()))
    pieces = lax.all_gather(stacked, "mp", axis=2, tiled=True)
    part_in = pieces[0]
    part_up = pieces[1]
    block = lax.dot_general(proj_in, part_up, over_tokens, preferred_element_type=jnp.float32)
    block = block + lax.dot_general(
        proj_up, part_in, over_tokens, preferred_element_type=jnp.float32
    )
    joined = jnp.concatenate([block, part_in.astype(jnp.float32)], 0)
    gram = joined[:slab]
    all_in = joined[slab:].astype(jnp.bfloat16)
    total = lax.psum(gram.astype(jnp.bfloat16), "dp").astype(jnp.float32)
    weighted = (kernel_of(own, ordered) * (0.5 * total)).astype(jnp.bfloat16)
    over_columns = (((1,), (1,)), ((), ()))
    mixed = lax.dot_general(all_in, weighted, over_columns, preferred_element_type=jnp.float32)
    factor = 2.0 / (lax.axis_size("dp") * inputs.shape[0])
    update = (proj_up.astype(jnp.float32) / jnp.sqrt(own)[None, :] + factor * mixed).astype(
        jnp.bfloat16
    )
    own_rows = lax.all_to_all(basis, "mp", split_axis=0, concat_axis=1, tiled=True)
    every_update = lax.all_gather(update, "mp", axis=1, tiled=True)
    result = lax.dot_general(
        own_rows, every_update, over_columns, preferred_element_type=jnp.float32
    )
    return result.astype(jnp.bfloat16)


def line_kernel(
    dims, ev, x_in, x_up, eig, out,
    ub, xb, pf, sup, sdn, rup, rdn, gz, gp, kb, so, ss, sr, zt, mx, ms, mr, uz, ff, fs, fa, fc, fb,
    ld_u, ld_x, up_s, up_r, dn_s, dn_r, zu_s, zd_s, z_r, p_s, p_r, c_s, c_r,
    m_s, m_r, wu_s, wd_s, w_r, f_s, f_r, o_s, o_r,
):
    R, C, tr, tc, tile, slab, tokens, parts, factor = dims
    q = slab // tile
    n = R * C
    rows = tr * tile
    d = lax.axis_index("dp")
    me = lax.axis_index("mp")
    r = me // C
    c = me % C
    partner = (1 - d, me)
    above = (d, (me + C) % n)
    below = (d, (me + n - C) % n)
    f32, bf16 = jnp.float32, jnp.bfloat16

    def span(i):
        return pl.ds(i * (tokens // parts), tokens // parts)

    def remote(src, dst, s_sem, r_sem, dev):
        return pltpu.make_async_remote_copy(
            src_ref=src, dst_ref=dst, send_sem=s_sem, recv_sem=r_sem,
            device_id=dev, device_id_type=pl.DeviceIdType.MESH,
        )

    def arrived(dst, r_sem):
        remote(dst, dst, c_s.at[0, 0], r_sem, partner).wait_recv()

    def left(src, s_sem):
        remote(src, src, s_sem, c_r.at[0, 0], partner).wait_send()

    barrier = pltpu.get_barrier_semaphore()
    for k in range(1, n):
        pl.semaphore_signal(
            barrier, inc=1, device_id=(d, (me + k) % n), device_id_type=pl.DeviceIdType.MESH
        )
    pl.semaphore_signal(
        barrier, inc=1, device_id=partner, device_id_type=pl.DeviceIdType.MESH
    )
    order = [R - 1, 0] + list(range(R - 2, 0, -1))
    for h, x in enumerate((x_in, x_up)):
        for la in range(tr):
            col = pl.multiple_of((la * R + r) * tile, tile)
            pltpu.make_async_copy(
                x.at[:, pl.ds(col, tile)], xb.at[h, :, la * tile:(la + 1) * tile], ld_x.at[h]
            ).start()
        if h == 0:
            for t in order:
                for k in range(q):
                    pltpu.make_async_copy(
                        eig.at[0, :, t * q + k],
                        ub.at[t, :, :, k * tile:(k + 1) * tile],
                        ld_u.at[t],
                    ).start()

    for h in range(2):
        pltpu.make_async_copy(xb.at[h], xb.at[h], ld_x.at[h]).wait()
        for t in order:
            if h == 0:
                pltpu.make_async_copy(ub.at[t], ub.at[t], ld_u.at[t]).wait()
            pf[h, t] = jnp.dot(
                xb[h], ub[t].reshape(rows, slab), preferred_element_type=f32
            )
            if h == 0 and t == order[0]:
                pl.semaphore_wait(barrier, n)
            if t > 0:
                @pl.when(r == 0)
                def _():
                    sup[h, t] = pf[h, t].astype(bf16)
                    remote(sup.at[h, t], rup.at[h, t], up_s.at[h, t], up_r.at[h, t], above).start()
            if t < R - 1:
                @pl.when(r == R - 1)
                def _():
                    sdn[h, t] = pf[h, t].astype(bf16)
                    remote(sdn.at[h, t], rdn.at[h, t], dn_s.at[h, t], dn_r.at[h, t], below).start()

    def relay_up(h):
        for t in range(R - 1, 0, -1):
            @pl.when((r > 0) & (r < t))
            def _():
                arrived(rup.at[h, t], up_r.at[h, t])
                sup[h, t] = (pf[h, t] + rup[h, t].astype(f32)).astype(bf16)
                remote(sup.at[h, t], rup.at[h, t], up_s.at[h, t], up_r.at[h, t], above).start()

    def relay_down(h):
        for t in range(R - 1):
            @pl.when((r < R - 1) & (r > t))
            def _():
                arrived(rdn.at[h, t], dn_r.at[h, t])
                sdn[h, t] = (pf[h, t] + rdn[h, t].astype(f32)).astype(bf16)
                remote(sdn.at[h, t], rdn.at[h, t], dn_s.at[h, t], dn_r.at[h, t], below).start()

    for h in range(2):
        @pl.when(r < R // 2)
        def _():
            relay_up(h)
            relay_down(h)

        @pl.when(r >= R // 2)
        def _():
            relay_down(h)
            relay_up(h)

        for t in range(R):
            @pl.when(r == t)
            def _():
                total = pf[h, t]
                if t > 0:
                    arrived(rup.at[h, t], up_r.at[h, t])
                    total = total + rup[h, t].astype(f32)
                if t < R - 1:
                    arrived(rdn.at[h, t], dn_r.at[h, t])
                    total = total + rdn[h, t].astype(f32)
                total = total.astype(bf16)
                gz[h, t] = total
                for i in range(parts):
                    buf = gz.at[h, t, span(i)]
                    if t < R - 1:
                        remote(buf, buf, zu_s.at[h, i, t], z_r.at[h, i, t], above).start()
                    if t > 0:
                        remote(buf, buf, zd_s.at[h, i, t], z_r.at[h, i, t], below).start()
                gp[h, c] = total
        for k in range(1, C):
            cc = (c + k) % C
            remote(
                gp.at[h, c], gp.at[h, c], p_s.at[h, k], p_r.at[h, c], (d, r * C + cc)
            ).start()

    def kernel_rows(lb, carry):
        row = jnp.sqrt(ev[pl.ds(lb * C + c, 1), :])
        sj = jnp.broadcast_to(row, (tile, tile)).T
        t = lb // q
        at = pl.multiple_of((lb % q) * tile, tile)
        for cc in range(C):
            for k in range(q):
                si = jnp.sqrt(ev[pl.ds((r * q + k) * C + cc, 1), :])
                kb[t, cc, pl.ds(at, tile), k * tile:(k + 1) * tile] = -0.5 / (si * sj * (si + sj))
        return carry

    lax.fori_loop(0, tc, kernel_rows, 0)

    def level(k, body):
        if k == 0:
            body(r, None)
        elif k < R:
            @pl.when(r >= k)
            def _():
                body(r - k, True)

            @pl.when(r + k < R)
            def _():
                body(r + k, False)

    def relay(buf, s, from_below, s_up, s_dn, r_sem):
        arrived(buf, r_sem)
        if from_below:
            @pl.when(r < R - 1)
            def _():
                remote(buf, buf, s_up, r_sem, above).start()
        else:
            @pl.when(r > 0)
            def _():
                remote(buf, buf, s_dn, r_sem, below).start()

    mx[...] = jnp.zeros_like(mx)

    def mixed_block(s, cc, carry):
        arrived(sr.at[s, cc], c_r.at[s, cc])
        weighted = (kb[s, cc] * (so[s, cc] + sr[s, cc].astype(f32))).astype(bf16)
        mx[cc] += jnp.dot(gz[0, s], weighted, preferred_element_type=f32)
        return carry

    def relay_piece(s, from_below):
        for h in range(2):
            for i in range(parts):
                relay(
                    gz.at[h, s, span(i)], s, from_below,
                    zu_s.at[h, i, s], zd_s.at[h, i, s], z_r.at[h, i, s],
                )

    def gram_piece(s, from_below):
        for h in range(2):
            zt[h] = gz[h, s].T

        def one(cc, carry):
            block = jnp.dot(zt[1], gp[0, cc], preferred_element_type=f32)
            block = block + jnp.dot(zt[0], gp[1, cc], preferred_element_type=f32)
            so[s, cc] = block
            ss[s, cc] = block.astype(bf16)
            remote(ss.at[s, cc], sr.at[s, cc], c_s.at[s, cc], c_r.at[s, cc], partner).start()
            return carry

        lax.fori_loop(0, C, one, 0)

    def mixed_piece(s, from_below):
        lax.fori_loop(0, C, functools.partial(mixed_block, s), 0)

    between = (r > 0) & (r < R - 1)

    def relay_first(k, body):
        @pl.when(between)
        def _():
            level(k, body)

    def relay_last(k, body):
        @pl.when((r == 0) | (r == R - 1))
        def _():
            level(k, body)

    relay_first(1, relay_piece)
    for h in range(2):
        for k in range(1, C):
            cc = (c + k) % C
            arrived(gp.at[h, cc], p_r.at[h, cc])
    for k in range(R):
        if k > 0:
            relay_first(k + 1, relay_piece)
        level(k, gram_piece)
        level(k, mixed_piece)
        relay_last(k + 1, relay_piece)

    for i in range(parts):
        for k in range(1, C):
            cc = (c + k) % C
            ms[cc, span(i)] = mx[cc, span(i)].astype(bf16)
            remote(
                ms.at[cc, span(i)], mr.at[c, span(i)], m_s.at[i, cc], m_r.at[i, c],
                (d, r * C + cc),
            ).start()
    roots = jnp.concatenate(
        [jnp.sqrt(ev[pl.ds((r * q + k) * C + c, 1), :]) for k in range(q)], axis=1
    )
    for i in range(parts):
        total = mx[c, span(i)]
        for k in range(1, C):
            cc = (c + k) % C
            arrived(mr.at[cc, span(i)], m_r.at[i, cc])
            total = total + mr[cc, span(i)].astype(f32)
        uz[r, span(i)] = (gz[1, r, span(i)].astype(f32) / roots + factor * total).astype(bf16)
        buf = uz.at[r, span(i)]

        @pl.when(r < R - 1)
        def _():
            remote(buf, buf, wu_s.at[i, r], w_r.at[i, r], above).start()

        @pl.when(r > 0)
        def _():
            remote(buf, buf, wd_s.at[i, r], w_r.at[i, r], below).start()

    ff[...] = jnp.zeros_like(ff)
    chunks = rows // slab

    def relay_update(s, from_below):
        for i in range(parts):
            relay(
                uz.at[s, span(i)], s, from_below, wu_s.at[i, s], wd_s.at[i, s], w_r.at[i, s]
            )

    def grad_piece(s, from_below):
        def one(i, carry):
            ff[i] += lax.dot_general(
                ub[s, pl.ds(i * q, q)].reshape(slab, slab), uz[s], (((1,), (1,)), ((), ())),
                preferred_element_type=f32,
            )
            return carry

        lax.fori_loop(0, chunks, one, 0)

    for k in range(R):
        if k > 0:
            relay_first(k + 1, relay_update)
        level(k, grad_piece)
        if k == 0:
            relay_first(1, relay_update)
        relay_last(k + 1, relay_update)

    half = C // 2
    for la in range(tr):
        place = (la % 2) * half + (la // 2) % half
        fs[la] = ff[la // q, (la % q) * tile:(la % q + 1) * tile, :].astype(bf16)

        @pl.when(c != place)
        def _():
            remote(
                fs.at[la], fa.at[la // C, c], f_s.at[la], f_r.at[la // C, c], (d, r * C + place)
            ).start()

    for j in range(tr // C):
        la = c // half + 2 * (c % half) + C * j
        total = fs[la].astype(f32)
        for k in range(1, C):
            cc = (c + k) % C
            arrived(fa.at[j, cc], f_r.at[j, cc])
            total = total + fa[j, cc].astype(f32)
        owner = (la * R + r) // q
        pos = (la * R + r) % q
        fc[j] = total.astype(bf16)

        @pl.when(owner == me)
        def _():
            fb[pos] = fc[j]

        @pl.when(owner != me)
        def _():
            remote(fc.at[j], fb.at[pos], o_s.at[j], o_r.at[pos], (d, owner)).start()

    for pos in range(q):
        g = me * q + pos
        la = g // R
        place = (la % 2) * half + (la // 2) % half

        @pl.when((g % R) * C + place != me)
        def _():
            arrived(fb.at[pos], o_r.at[pos])

        out[pos * tile:(pos + 1) * tile, :] = fb[pos]

    for h in range(2):
        for t in range(R):
            if t > 0:
                @pl.when(r < t)
                def _():
                    left(sup.at[h, t], up_s.at[h, t])
            if t < R - 1:
                @pl.when(r > t)
                def _():
                    left(sdn.at[h, t], dn_s.at[h, t])

            for i in range(parts):
                @pl.when((r >= t) & (r < R - 1))
                def _():
                    left(gz.at[h, t, span(i)], zu_s.at[h, i, t])

                @pl.when((r <= t) & (r > 0))
                def _():
                    left(gz.at[h, t, span(i)], zd_s.at[h, i, t])
        for k in range(1, C):
            left(gp.at[h, c], p_s.at[h, k])
    for t in range(R):
        for i in range(parts):
            @pl.when((r >= t) & (r < R - 1))
            def _():
                left(uz.at[t, span(i)], wu_s.at[i, t])

            @pl.when((r <= t) & (r > 0))
            def _():
                left(uz.at[t, span(i)], wd_s.at[i, t])
        for cc in range(C):
            left(ss.at[t, cc], c_s.at[t, cc])
    for k in range(1, C):
        cc = (c + k) % C
        for i in range(parts):
            left(ms.at[cc, span(i)], m_s.at[i, cc])
    for la in range(tr):
        @pl.when(c != (la % 2) * half + (la // 2) % half)
        def _():
            left(fs.at[la], f_s.at[la])
    for j in range(tr // C):
        la = c // half + 2 * (c % half) + C * j

        @pl.when((la * R + r) // q != me)
        def _():
            left(fc.at[j], o_s.at[j])


def grid_on_device(R, C, inputs, upstream, eig_tiles, eigvals):
    _, tr, tc, tile, _ = eig_tiles.shape
    tokens, width = inputs.shape
    slab = width // (R * C)
    q = slab // tile
    parts = 4 if tokens % 64 == 0 else 1
    rows = tr * tile
    factor = 2.0 / (lax.axis_size("dp") * tokens)
    bf16, f32 = jnp.bfloat16, jnp.float32
    dma = pltpu.SemaphoreType.DMA
    piece = (tokens, slab)
    scratch = [
        pltpu.VMEM((R, tr, tile, slab), bf16),
        pltpu.VMEM((2, tokens, rows), bf16),
        pltpu.VMEM((2, R) + piece, f32),
        pltpu.VMEM((2, R) + piece, bf16),
        pltpu.VMEM((2, R) + piece, bf16),
        pltpu.VMEM((2, R) + piece, bf16),
        pltpu.VMEM((2, R) + piece, bf16),
        pltpu.VMEM((2, R) + piece, bf16),
        pltpu.VMEM((2, C) + piece, bf16),
        pltpu.VMEM((R, C, slab, slab), f32),
        pltpu.VMEM((R, C, slab, slab), f32),
        pltpu.VMEM((R, C, slab, slab), bf16),
        pltpu.VMEM((R, C, slab, slab), bf16),
        pltpu.VMEM((2, slab, tokens), bf16),
        pltpu.VMEM((C,) + piece, f32),
        pltpu.VMEM((C,) + piece, bf16),
        pltpu.VMEM((C,) + piece, bf16),
        pltpu.VMEM((R,) + piece, bf16),
        pltpu.VMEM((rows // slab, slab, tokens), f32),
        pltpu.VMEM((tr, tile, tokens), bf16),
        pltpu.VMEM((tr // C, C, tile, tokens), bf16),
        pltpu.VMEM((tr // C, tile, tokens), bf16),
        pltpu.VMEM((q, tile, tokens), bf16),
        dma((R,)), dma((2,)),
        dma((2, R)), dma((2, R)), dma((2, R)), dma((2, R)),
        dma((2, parts, R)), dma((2, parts, R)), dma((2, parts, R)),
        dma((2, C)), dma((2, C)),
        dma((R, C)), dma((R, C)),
        dma((parts, C)), dma((parts, C)),
        dma((parts, R)), dma((parts, R)), dma((parts, R)),
        dma((tr,)), dma((tr // C, C)), dma((tr // C,)), dma((q,)),
    ]
    anywhere = pl.BlockSpec(memory_space=pltpu.HBM)
    return pl.pallas_call(
        functools.partial(line_kernel, (R, C, tr, tc, tile, slab, tokens, parts, factor)),
        out_shape=jax.ShapeDtypeStruct((slab, tokens), bf16),
        in_specs=[pl.BlockSpec(memory_space=pltpu.VMEM), anywhere, anywhere, anywhere],
        out_specs=pl.BlockSpec(memory_space=pltpu.VMEM),
        scratch_shapes=scratch,
        compiler_params=pltpu.CompilerParams(
            collective_id=0, has_side_effects=True, vmem_limit_bytes=65_800_000
        ),
    )(eigvals.reshape(width // tile, tile), inputs, upstream, eig_tiles)


def body(inputs, upstream, eig_tiles, eigvals):
    width = inputs.shape[1]
    groups = lax.axis_size("mp")
    _, tr, tc, tile, _ = eig_tiles.shape
    R = width // (tr * tile)
    C = groups // R
    slab = width // groups
    whole_tiles = slab % tile == 0 and (tr * tile) % slab == 0 and tc % R == 0
    if lax.axis_size("dp") == 2 and whole_tiles and R > 1 and C % 2 == 0 and tr % C == 0:
        return grid_on_device(R, C, inputs, upstream, eig_tiles, eigvals)
    return on_device(inputs, upstream, eig_tiles, eigvals)


def solution(mesh):
    return jax.shard_map(
        body,
        mesh=mesh,
        in_specs=(P("dp", None), P("dp", None), P("mp", None, None, None, None), P()),
        out_specs=P("mp", "dp"),
        check_vma=False,
    )
```

```python
import functools

import jax
import jax.numpy as jnp
from jax import lax
from jax.experimental import pallas as pl
from jax.experimental.pallas import tpu as pltpu
from jax.sharding import PartitionSpec as P


def kernel_of(left, right):
    root_left = jnp.sqrt(left)[:, None]
    root_right = jnp.sqrt(right)[None, :]
    return -1.0 / (root_left * root_right * (root_left + root_right))


def on_device(inputs, upstream, eig_tiles, eigvals):
    groups = lax.axis_size("mp")
    member = lax.axis_index("mp")
    width = eigvals.shape[0]
    slab = width // groups
    tile_rows = eig_tiles.shape[1]
    tile_cols = eig_tiles.shape[2]
    tile = eig_tiles.shape[3]
    grid_rows = width // (tile_rows * tile)
    grid_cols = groups // grid_rows
    piece = tile_cols * tile // groups
    local = jnp.transpose(eig_tiles[0], (0, 2, 1, 3)).reshape(tile_rows * tile, groups, piece)
    moved = lax.all_to_all(local, "mp", split_axis=1, concat_axis=1, tiled=True)
    moved = moved.reshape(tile_rows, tile, grid_rows, grid_cols, piece)
    basis = jnp.transpose(moved, (0, 2, 1, 3, 4)).reshape(width, slab)
    ordered = jnp.transpose(eigvals.reshape(tile_cols, grid_cols, tile), (1, 0, 2)).reshape(
        grid_cols, groups, piece
    )
    ordered = jnp.transpose(ordered, (1, 0, 2)).reshape(width)
    own = lax.dynamic_slice_in_dim(ordered, member * slab, slab)
    proj_in = jnp.dot(inputs, basis, preferred_element_type=jnp.float32).astype(jnp.bfloat16)
    proj_up = jnp.dot(upstream, basis, preferred_element_type=jnp.float32).astype(jnp.bfloat16)
    stacked = jnp.stack([proj_in, proj_up], 0)
    over_tokens = (((0,), (0,)), ((), ()))
    pieces = lax.all_gather(stacked, "mp", axis=2, tiled=True)
    part_in = pieces[0]
    part_up = pieces[1]
    block = lax.dot_general(proj_in, part_up, over_tokens, preferred_element_type=jnp.float32)
    block = block + lax.dot_general(
        proj_up, part_in, over_tokens, preferred_element_type=jnp.float32
    )
    joined = jnp.concatenate([block, part_in.astype(jnp.float32)], 0)
    gram = joined[:slab]
    all_in = joined[slab:].astype(jnp.bfloat16)
    total = lax.psum(gram.astype(jnp.bfloat16), "dp").astype(jnp.float32)
    weighted = (kernel_of(own, ordered) * (0.5 * total)).astype(jnp.bfloat16)
    over_columns = (((1,), (1,)), ((), ()))
    mixed = lax.dot_general(all_in, weighted, over_columns, preferred_element_type=jnp.float32)
    factor = 2.0 / (lax.axis_size("dp") * inputs.shape[0])
    update = (proj_up.astype(jnp.float32) / jnp.sqrt(own)[None, :] + factor * mixed).astype(
        jnp.bfloat16
    )
    own_rows = lax.all_to_all(basis, "mp", split_axis=0, concat_axis=1, tiled=True)
    every_update = lax.all_gather(update, "mp", axis=1, tiled=True)
    result = lax.dot_general(
        own_rows, every_update, over_columns, preferred_element_type=jnp.float32
    )
    return result.astype(jnp.bfloat16)


def line_kernel(
    dims, ev, x_in, x_up, eig, out,
    ub, xb, pf, sup, sdn, rup, rdn, gz, gp, kb, so, ss, sr, zt, mx, ms, mr, uz, ff, fs, fa, fc, fb,
    ld_u, ld_x, up_s, up_r, dn_s, dn_r, zu_s, zd_s, z_r, p_s, p_r, c_s, c_r,
    m_s, m_r, wu_s, wd_s, w_r, f_s, f_r, o_s, o_r,
):
    R, C, tr, tc, tile, slab, tokens, parts, factor = dims
    q = slab // tile
    n = R * C
    rows = tr * tile
    d = lax.axis_index("dp")
    me = lax.axis_index("mp")
    r = me // C
    c = me % C
    partner = (1 - d, me)
    above = (d, (me + C) % n)
    below = (d, (me + n - C) % n)
    f32, bf16 = jnp.float32, jnp.bfloat16

    def span(i):
        return pl.ds(i * (tokens // parts), tokens // parts)

    def remote(src, dst, s_sem, r_sem, dev):
        return pltpu.make_async_remote_copy(
            src_ref=src, dst_ref=dst, send_sem=s_sem, recv_sem=r_sem,
            device_id=dev, device_id_type=pl.DeviceIdType.MESH,
        )

    def arrived(dst, r_sem):
        remote(dst, dst, c_s.at[0, 0], r_sem, partner).wait_recv()

    def left(src, s_sem):
        remote(src, src, s_sem, c_r.at[0, 0], partner).wait_send()

    barrier = pltpu.get_barrier_semaphore()
    for k in range(1, n):
        pl.semaphore_signal(
            barrier, inc=1, device_id=(d, (me + k) % n), device_id_type=pl.DeviceIdType.MESH
        )
    pl.semaphore_signal(
        barrier, inc=1, device_id=partner, device_id_type=pl.DeviceIdType.MESH
    )
    order = [R - 1, 0] + list(range(R - 2, 0, -1))
    for h, x in enumerate((x_in, x_up)):
        for la in range(tr):
            col = pl.multiple_of((la * R + r) * tile, tile)
            pltpu.make_async_copy(
                x.at[:, pl.ds(col, tile)], xb.at[h, :, la * tile:(la + 1) * tile], ld_x.at[h]
            ).start()
        if h == 0:
            for t in order:
                for k in range(q):
                    pltpu.make_async_copy(
                        eig.at[0, :, t * q + k],
                        ub.at[t, :, :, k * tile:(k + 1) * tile],
                        ld_u.at[t],
                    ).start()

    for h in range(2):
        pltpu.make_async_copy(xb.at[h], xb.at[h], ld_x.at[h]).wait()
        for t in order:
            if h == 0:
                pltpu.make_async_copy(ub.at[t], ub.at[t], ld_u.at[t]).wait()
            pf[h, t] = jnp.dot(
                xb[h], ub[t].reshape(rows, slab), preferred_element_type=f32
            )
            if h == 0 and t == order[0]:
                pl.semaphore_wait(barrier, n)
            if t > 0:
                @pl.when(r == 0)
                def _():
                    sup[h, t] = pf[h, t].astype(bf16)
                    remote(sup.at[h, t], rup.at[h, t], up_s.at[h, t], up_r.at[h, t], above).start()
            if t < R - 1:
                @pl.when(r == R - 1)
                def _():
                    sdn[h, t] = pf[h, t].astype(bf16)
                    remote(sdn.at[h, t], rdn.at[h, t], dn_s.at[h, t], dn_r.at[h, t], below).start()

    def relay_up(h):
        for t in range(R - 1, 0, -1):
            @pl.when((r > 0) & (r < t))
            def _():
                arrived(rup.at[h, t], up_r.at[h, t])
                sup[h, t] = (pf[h, t] + rup[h, t].astype(f32)).astype(bf16)
                remote(sup.at[h, t], rup.at[h, t], up_s.at[h, t], up_r.at[h, t], above).start()

    def relay_down(h):
        for t in range(R - 1):
            @pl.when((r < R - 1) & (r > t))
            def _():
                arrived(rdn.at[h, t], dn_r.at[h, t])
                sdn[h, t] = (pf[h, t] + rdn[h, t].astype(f32)).astype(bf16)
                remote(sdn.at[h, t], rdn.at[h, t], dn_s.at[h, t], dn_r.at[h, t], below).start()

    for h in range(2):
        @pl.when(r < R // 2)
        def _():
            relay_up(h)
            relay_down(h)

        @pl.when(r >= R // 2)
        def _():
            relay_down(h)
            relay_up(h)

        for t in range(R):
            @pl.when(r == t)
            def _():
                total = pf[h, t]
                if t > 0:
                    arrived(rup.at[h, t], up_r.at[h, t])
                    total = total + rup[h, t].astype(f32)
                if t < R - 1:
                    arrived(rdn.at[h, t], dn_r.at[h, t])
                    total = total + rdn[h, t].astype(f32)
                total = total.astype(bf16)
                gz[h, t] = total
                for i in range(parts):
                    buf = gz.at[h, t, span(i)]
                    if t < R - 1:
                        remote(buf, buf, zu_s.at[h, i, t], z_r.at[h, i, t], above).start()
                    if t > 0:
                        remote(buf, buf, zd_s.at[h, i, t], z_r.at[h, i, t], below).start()
                gp[h, c] = total
        for k in range(1, C):
            cc = (c + k) % C
            remote(
                gp.at[h, c], gp.at[h, c], p_s.at[h, k], p_r.at[h, c], (d, r * C + cc)
            ).start()

    def kernel_rows(lb, carry):
        row = jnp.sqrt(ev[pl.ds(lb * C + c, 1), :])
        sj = jnp.broadcast_to(row, (tile, tile)).T
        t = lb // q
        at = pl.multiple_of((lb % q) * tile, tile)
        for cc in range(C):
            for k in range(q):
                si = jnp.sqrt(ev[pl.ds((r * q + k) * C + cc, 1), :])
                kb[t, cc, pl.ds(at, tile), k * tile:(k + 1) * tile] = -0.5 / (si * sj * (si + sj))
        return carry

    lax.fori_loop(0, tc, kernel_rows, 0, unroll=2)

    def level(k, body):
        if k == 0:
            body(r, None)
        elif k < R:
            @pl.when(r >= k)
            def _():
                body(r - k, True)

            @pl.when(r + k < R)
            def _():
                body(r + k, False)

    def relay(buf, s, from_below, s_up, s_dn, r_sem):
        arrived(buf, r_sem)
        if from_below:
            @pl.when(r < R - 1)
            def _():
                remote(buf, buf, s_up, r_sem, above).start()
        else:
            @pl.when(r > 0)
            def _():
                remote(buf, buf, s_dn, r_sem, below).start()

    mx[...] = jnp.zeros_like(mx)

    def mixed_block(s, cc, carry):
        arrived(sr.at[s, cc], c_r.at[s, cc])
        weighted = (kb[s, cc] * (so[s, cc] + sr[s, cc].astype(f32))).astype(bf16)
        mx[cc] += jnp.dot(gz[0, s], weighted, preferred_element_type=f32)
        return carry

    def relay_piece(s, from_below):
        for h in range(2):
            for i in range(parts):
                relay(
                    gz.at[h, s, span(i)], s, from_below,
                    zu_s.at[h, i, s], zd_s.at[h, i, s], z_r.at[h, i, s],
                )

    def gram_piece(s, from_below):
        for h in range(2):
            zt[h] = gz[h, s].T

        def one(cc, carry):
            block = jnp.dot(zt[1], gp[0, cc], preferred_element_type=f32)
            block = block + jnp.dot(zt[0], gp[1, cc], preferred_element_type=f32)
            so[s, cc] = block
            ss[s, cc] = block.astype(bf16)
            remote(ss.at[s, cc], sr.at[s, cc], c_s.at[s, cc], c_r.at[s, cc], partner).start()
            return carry

        lax.fori_loop(0, C, one, 0, unroll=True)

    def mixed_piece(s, from_below):
        lax.fori_loop(0, C, functools.partial(mixed_block, s), 0, unroll=True)

    between = (r > 0) & (r < R - 1)

    def relay_first(k, body):
        @pl.when(between)
        def _():
            level(k, body)

    def relay_last(k, body):
        @pl.when((r == 0) | (r == R - 1))
        def _():
            level(k, body)

    relay_first(1, relay_piece)
    for h in range(2):
        for k in range(1, C):
            cc = (c + k) % C
            arrived(gp.at[h, cc], p_r.at[h, cc])
    for k in range(R):
        if k > 0:
            relay_first(k + 1, relay_piece)
        level(k, gram_piece)
        level(k, mixed_piece)
        relay_last(k + 1, relay_piece)

    for i in range(parts):
        for k in range(1, C):
            cc = (c + k) % C
            ms[cc, span(i)] = mx[cc, span(i)].astype(bf16)
            remote(
                ms.at[cc, span(i)], mr.at[c, span(i)], m_s.at[i, cc], m_r.at[i, c],
                (d, r * C + cc),
            ).start()
    roots = jnp.concatenate(
        [jnp.sqrt(ev[pl.ds((r * q + k) * C + c, 1), :]) for k in range(q)], axis=1
    )
    for i in range(parts):
        total = mx[c, span(i)]
        for k in range(1, C):
            cc = (c + k) % C
            arrived(mr.at[cc, span(i)], m_r.at[i, cc])
            total = total + mr[cc, span(i)].astype(f32)
        uz[r, span(i)] = (gz[1, r, span(i)].astype(f32) / roots + factor * total).astype(bf16)
        buf = uz.at[r, span(i)]

        @pl.when(r < R - 1)
        def _():
            remote(buf, buf, wu_s.at[i, r], w_r.at[i, r], above).start()

        @pl.when(r > 0)
        def _():
            remote(buf, buf, wd_s.at[i, r], w_r.at[i, r], below).start()

    ff[...] = jnp.zeros_like(ff)
    chunks = rows // slab

    def relay_update(s, from_below):
        for i in range(parts):
            relay(
                uz.at[s, span(i)], s, from_below, wu_s.at[i, s], wd_s.at[i, s], w_r.at[i, s]
            )

    def grad_piece(s, from_below):
        def one(i, carry):
            ff[i] += lax.dot_general(
                ub[s, pl.ds(i * q, q)].reshape(slab, slab), uz[s], (((1,), (1,)), ((), ())),
                preferred_element_type=f32,
            )
            return carry

        lax.fori_loop(0, chunks, one, 0, unroll=True)

    for k in range(R):
        if k > 0:
            relay_first(k + 1, relay_update)
        level(k, grad_piece)
        if k == 0:
            relay_first(1, relay_update)
        relay_last(k + 1, relay_update)

    half = C // 2
    for la in range(tr):
        place = (la % 2) * half + (la // 2) % half
        fs[la] = ff[la // q, (la % q) * tile:(la % q + 1) * tile, :].astype(bf16)

        @pl.when(c != place)
        def _():
            remote(
                fs.at[la], fa.at[la // C, c], f_s.at[la], f_r.at[la // C, c], (d, r * C + place)
            ).start()

    for j in range(tr // C):
        la = c // half + 2 * (c % half) + C * j
        total = fs[la].astype(f32)
        for k in range(1, C):
            cc = (c + k) % C
            arrived(fa.at[j, cc], f_r.at[j, cc])
            total = total + fa[j, cc].astype(f32)
        owner = (la * R + r) // q
        pos = (la * R + r) % q
        fc[j] = total.astype(bf16)

        @pl.when(owner == me)
        def _():
            fb[pos] = fc[j]

        @pl.when(owner != me)
        def _():
            remote(fc.at[j], fb.at[pos], o_s.at[j], o_r.at[pos], (d, owner)).start()

    for pos in range(q):
        g = me * q + pos
        la = g // R
        place = (la % 2) * half + (la // 2) % half

        @pl.when((g % R) * C + place != me)
        def _():
            arrived(fb.at[pos], o_r.at[pos])

        out[pos * tile:(pos + 1) * tile, :] = fb[pos]

    for h in range(2):
        for t in range(R):
            if t > 0:
                @pl.when(r < t)
                def _():
                    left(sup.at[h, t], up_s.at[h, t])
            if t < R - 1:
                @pl.when(r > t)
                def _():
                    left(sdn.at[h, t], dn_s.at[h, t])

            for i in range(parts):
                @pl.when((r >= t) & (r < R - 1))
                def _():
                    left(gz.at[h, t, span(i)], zu_s.at[h, i, t])

                @pl.when((r <= t) & (r > 0))
                def _():
                    left(gz.at[h, t, span(i)], zd_s.at[h, i, t])
        for k in range(1, C):
            left(gp.at[h, c], p_s.at[h, k])
    for t in range(R):
        for i in range(parts):
            @pl.when((r >= t) & (r < R - 1))
            def _():
                left(uz.at[t, span(i)], wu_s.at[i, t])

            @pl.when((r <= t) & (r > 0))
            def _():
                left(uz.at[t, span(i)], wd_s.at[i, t])
        for cc in range(C):
            left(ss.at[t, cc], c_s.at[t, cc])
    for k in range(1, C):
        cc = (c + k) % C
        for i in range(parts):
            left(ms.at[cc, span(i)], m_s.at[i, cc])
    for la in range(tr):
        @pl.when(c != (la % 2) * half + (la // 2) % half)
        def _():
            left(fs.at[la], f_s.at[la])
    for j in range(tr // C):
        la = c // half + 2 * (c % half) + C * j

        @pl.when((la * R + r) // q != me)
        def _():
            left(fc.at[j], o_s.at[j])


def grid_on_device(R, C, inputs, upstream, eig_tiles, eigvals):
    _, tr, tc, tile, _ = eig_tiles.shape
    tokens, width = inputs.shape
    slab = width // (R * C)
    q = slab // tile
    parts = 4 if tokens % 64 == 0 else 1
    rows = tr * tile
    factor = 2.0 / (lax.axis_size("dp") * tokens)
    bf16, f32 = jnp.bfloat16, jnp.float32
    dma = pltpu.SemaphoreType.DMA
    piece = (tokens, slab)
    scratch = [
        pltpu.VMEM((R, tr, tile, slab), bf16),
        pltpu.VMEM((2, tokens, rows), bf16),
        pltpu.VMEM((2, R) + piece, f32),
        pltpu.VMEM((2, R) + piece, bf16),
        pltpu.VMEM((2, R) + piece, bf16),
        pltpu.VMEM((2, R) + piece, bf16),
        pltpu.VMEM((2, R) + piece, bf16),
        pltpu.VMEM((2, R) + piece, bf16),
        pltpu.VMEM((2, C) + piece, bf16),
        pltpu.VMEM((R, C, slab, slab), f32),
        pltpu.VMEM((R, C, slab, slab), f32),
        pltpu.VMEM((R, C, slab, slab), bf16),
        pltpu.VMEM((R, C, slab, slab), bf16),
        pltpu.VMEM((2, slab, tokens), bf16),
        pltpu.VMEM((C,) + piece, f32),
        pltpu.VMEM((C,) + piece, bf16),
        pltpu.VMEM((C,) + piece, bf16),
        pltpu.VMEM((R,) + piece, bf16),
        pltpu.VMEM((rows // slab, slab, tokens), f32),
        pltpu.VMEM((tr, tile, tokens), bf16),
        pltpu.VMEM((tr // C, C, tile, tokens), bf16),
        pltpu.VMEM((tr // C, tile, tokens), bf16),
        pltpu.VMEM((q, tile, tokens), bf16),
        dma((R,)), dma((2,)),
        dma((2, R)), dma((2, R)), dma((2, R)), dma((2, R)),
        dma((2, parts, R)), dma((2, parts, R)), dma((2, parts, R)),
        dma((2, C)), dma((2, C)),
        dma((R, C)), dma((R, C)),
        dma((parts, C)), dma((parts, C)),
        dma((parts, R)), dma((parts, R)), dma((parts, R)),
        dma((tr,)), dma((tr // C, C)), dma((tr // C,)), dma((q,)),
    ]
    anywhere = pl.BlockSpec(memory_space=pltpu.HBM)
    return pl.pallas_call(
        functools.partial(line_kernel, (R, C, tr, tc, tile, slab, tokens, parts, factor)),
        out_shape=jax.ShapeDtypeStruct((slab, tokens), bf16),
        in_specs=[pl.BlockSpec(memory_space=pltpu.VMEM), anywhere, anywhere, anywhere],
        out_specs=pl.BlockSpec(memory_space=pltpu.VMEM),
        scratch_shapes=scratch,
        compiler_params=pltpu.CompilerParams(
            collective_id=0, has_side_effects=True, vmem_limit_bytes=65_800_000
        ),
    )(eigvals.reshape(width // tile, tile), inputs, upstream, eig_tiles)


def body(inputs, upstream, eig_tiles, eigvals):
    width = inputs.shape[1]
    groups = lax.axis_size("mp")
    _, tr, tc, tile, _ = eig_tiles.shape
    R = width // (tr * tile)
    C = groups // R
    slab = width // groups
    whole_tiles = slab % tile == 0 and (tr * tile) % slab == 0 and tc % R == 0
    if lax.axis_size("dp") == 2 and whole_tiles and R > 1 and C % 2 == 0 and tr % C == 0:
        return grid_on_device(R, C, inputs, upstream, eig_tiles, eigvals)
    return on_device(inputs, upstream, eig_tiles, eigvals)


def solution(mesh):
    return jax.shard_map(
        body,
        mesh=mesh,
        in_specs=(P("dp", None), P("dp", None), P("mp", None, None, None, None), P()),
        out_specs=P("mp", "dp"),
        check_vma=False,
    )
```
